1024 devices in a mesh: group: 128 (over z_lo, y, core), dev: 8 (over z_hi, x).
Axes of the slice: x: 4, y: 4, z: 32 (z_hi: 2, z_lo: 16; z = z_hi * 16 + z_lo), core: 2. Of those that a mesh axis runs over, the one named last changes fastest.
Arguments:
- initial_dofs: float32 [56, 9, 32768], P(None, None, ('group', 'dev')), may hold values from -6 to 6
- jacobians: float32 [3, 9, 9, 32768], P(None, None, None, ('group', 'dev')), may hold values from -0.9 to 0.9
- stiffness: float32 [3, 56, 56], replicated, may hold values from -0.75 to 0.75
- projection: float32 [4, 21, 56], replicated, may hold values from -0.75 to 0.75
- minus_root: float32 [4, 9, 9, 32768], P(None, None, None, ('group', 'dev')), may hold values from -1.2 to 1.2
- plus_flux: float32 [4, 9, 9, 32768], P(None, None, None, ('group', 'dev')), may hold values from -0.9 to 0.9
- cluster_id: int32 [32768], P(('group', 'dev')), may hold values from 0 to 2, as said below
- neighbours: int32 [2, 4, 32768], P(None, None, ('group', 'dev')), may hold values from 0 to 159, as said below
- send_faces: int32 [4, 8192], P(None, ('group', 'dev')), may hold values from 0 to 127, as said below
Outputs:
- final_dofs: float32 [56, 9, 32768], P(None, None, ('group', 'dev'))
The draws below stay inside these ranges and needn't reach their ends.
Inputs may be any that keep to these rules, and one draw needn't show every extreme that they name: `cluster_id`: the 32 consecutive tetrahedra of each partition hold at most 16 of cluster 2, and some partition holds exactly 16. `neighbours`: row 0: for face f of tetrahedron e, either f2 * 32 + e2 naming face f2 of tetrahedron e2 of the same partition (the pairing is symmetric), or 128 + p * 8 + s naming slot s of direction p (0: group index - 1, 1: group index + 1, 2: dev index - 1, 3: dev index + 1); in each partition every slot is named by exactly one face. Row 1: the face number of the adjoining face in its own tetrahedron. `send_faces`: entry (p, s) of a partition is f * 32 + e for its face f of tetrahedron e whose row 0 code is 128 + p * 8 + s; that face adjoins the face at entry (opposite of p, s) of the partition in direction p.
All inputs are finite; a program needn't handle non-finite values.
Results may differ from the reference program's by a relative error of at most 0.0003.
Values sent between devices are 32-bit elements; how exact they have to be, the bound alone decides.
A program may use at most 128 MiB of HBM per device.

```python
import jax
import jax.numpy as jnp
from jax import lax

MODES = 56
FACES = 21
QUANT = 9
TERMS = 6
MACRO = 1
ELEM_DEV = 32
SLOTS = 8
FAST_MAX = 16
ELEMS = 32768
N_GROUP = 128
N_DEV = 8


def mesh_tables(key):
    device_total = N_GROUP * N_DEV
    face_total = 4 * ELEM_DEV
    remote_total = 4 * SLOTS
    device_keys = jax.random.split(jax.random.fold_in(key, 17), device_total)
    face_orders = jax.vmap(lambda single: jax.random.permutation(single, face_total))(device_keys).astype(jnp.int32)
    outgoing = face_orders[:, :remote_total]
    partners = face_orders[:, remote_total:].reshape(device_total, -1, 2)
    pair_left = partners[:, :, 0]
    pair_right = partners[:, :, 1]
    slot_codes = face_total + jnp.arange(remote_total, dtype=jnp.int32)

    def codes_for(out_row, left_row, right_row):
        lookup = jnp.zeros((face_total,), jnp.int32)
        lookup = lookup.at[out_row].set(slot_codes)
        lookup = lookup.at[left_row].set(right_row)
        lookup = lookup.at[right_row].set(left_row)
        return lookup
    face_codes = jax.vmap(codes_for)(outgoing, pair_left, pair_right)
    slot_grid = outgoing.reshape(N_GROUP, N_DEV, 4, SLOTS)
    from_peer = jnp.stack([jnp.roll(slot_grid[:, :, 1], 1, axis=0), jnp.roll(slot_grid[:, :, 0], -1, axis=0), jnp.roll(slot_grid[:, :, 3], 1, axis=1), jnp.roll(slot_grid[:, :, 2], -1, axis=1)], axis=2).reshape(device_total, remote_total)
    peer_face = from_peer // ELEM_DEV

    def faces_for(out_row, left_row, right_row, peer_row):
        lookup = jnp.zeros((face_total,), jnp.int32)
        lookup = lookup.at[out_row].set(peer_row)
        lookup = lookup.at[left_row].set(right_row // ELEM_DEV)
        lookup = lookup.at[right_row].set(left_row // ELEM_DEV)
        return lookup
    neighbour_faces = jax.vmap(faces_for)(outgoing, pair_left, pair_right, peer_face)

    def spread(lookup):
        return lookup.reshape(device_total, 4, ELEM_DEV).transpose(1, 0, 2).reshape(4, device_total * ELEM_DEV)
    neighbour_table = jnp.stack([spread(face_codes), spread(neighbour_faces)]).astype(jnp.int32)
    send_table = outgoing.reshape(device_total, 4, SLOTS).transpose(1, 0, 2).reshape(4, device_total * SLOTS).astype(jnp.int32)
    return (neighbour_table, send_table)


def draw_neighbours(key, part):
    return mesh_tables(key)[0]


def draw_send_faces(key, part):
    return mesh_tables(key)[1]


def draw_cluster_id(key, part):
    device_total = N_GROUP * N_DEV
    key_root, key_busy, key_rank, key_middle = jax.random.split(jax.random.fold_in(key, 29), 4)
    draws_root = jax.random.randint(key_root, (device_total,), 0, FAST_MAX + 1)
    fast_count = draws_root * draws_root // FAST_MAX
    busiest = jax.random.randint(key_busy, (), 0, device_total)
    fast_count = jnp.where(jnp.arange(device_total) == busiest, FAST_MAX, fast_count)
    position_rank = jax.vmap(lambda single: jax.random.permutation(single, ELEM_DEV))(jax.random.split(key_rank, device_total))
    is_fast = position_rank < fast_count[:, None]
    middle = jax.random.randint(key_middle, (device_total, ELEM_DEV), 0, 2)
    return jnp.where(is_fast, 2, middle).reshape(device_total * ELEM_DEV).astype(jnp.int32)


def block_scale(stream_key, shape, cuts, low, high):
    def one(axis_at, shards_of):
        draws = jax.random.uniform(jax.random.fold_in(jax.random.fold_in(stream_key, 6), axis_at), (shards_of,), jnp.float32, low / len(cuts), high / len(cuts))
        return jnp.repeat(jnp.exp(draws), shape[axis_at] // shards_of).reshape((-1,) + (1,) * (len(shape) - axis_at - 1))

    gain = one(*cuts[0])
    for cut in cuts[1:]:
        gain = gain * one(*cut)
    return gain


def centred(stream_key, shape, scale, reach, pieces=(), held_as=jnp.bfloat16):
    values = jax.random.normal(stream_key, shape, jnp.float32) * scale
    if len(pieces) > 0:
        values = block_scale(stream_key, shape, pieces, -0.22, 0.18) * values
    return jnp.clip(values, min=-reach, max=reach).astype(held_as)


def setup_inputs(seed: int = 0) -> dict:
    keys = jax.random.split(jax.random.key(seed), 10)
    initial_dofs = centred(keys[0], (MODES, QUANT, ELEMS), 1.0, 6.0, ((2, 1024),), jnp.float32)
    jacobians = centred(keys[1], (3, QUANT, QUANT, ELEMS), 0.15, 0.9, ((3, 1024),), jnp.float32)
    stiffness = centred(keys[2], (3, MODES, MODES), MODES ** -0.5, 0.75, (), jnp.float32)
    projection = centred(keys[3], (4, FACES, MODES), MODES ** -0.5, 0.75, (), jnp.float32)
    minus_root = centred(keys[4], (4, QUANT, QUANT, ELEMS), 0.2, 1.2, ((3, 1024),), jnp.float32)
    plus_flux = centred(keys[5], (4, QUANT, QUANT, ELEMS), 0.15, 0.9, ((3, 1024),), jnp.float32)
    cluster_id = draw_cluster_id(jax.random.fold_in(keys[9], 71), 0)
    neighbours = draw_neighbours(jax.random.fold_in(keys[9], 71), 0)
    send_faces = draw_send_faces(jax.random.fold_in(keys[9], 71), 0)
    return {"initial_dofs": initial_dofs, "jacobians": jacobians, "stiffness": stiffness, "projection": projection, "minus_root": minus_root, "plus_flux": plus_flux, "cluster_id": cluster_id, "neighbours": neighbours, "send_faces": send_faces}


precise = lax.Precision.HIGHEST


def contract_small(left, right):
    inner = left.shape[-2]
    total = left[..., 0, None, :] * right[..., 0, :, :]
    for index in range(1, inner):
        total = total + left[..., index, None, :] * right[..., index, :, :]
    return total


def apply_operator(values, stiffness_op, star_set):
    mode_count, quantity_count, element_count = values.shape
    rotated = jnp.dot(stiffness_op, values.reshape(mode_count, quantity_count * element_count), precision=precise)
    rotated = rotated.reshape(3, mode_count, quantity_count, element_count)
    total = contract_small(rotated[0], star_set[0][None])
    total = total + contract_small(rotated[1], star_set[1][None])
    total = total + contract_small(rotated[2], star_set[2][None])
    return total


def expansion(values, stiffness_op, star_set):
    series = [values]
    for power in range(TERMS - 1):
        series.append(apply_operator(series[-1], stiffness_op, star_set))
    return jnp.stack(series)


def coefficients(offsets):
    start_time = offsets * 0.25
    end_time = start_time + 0.25
    series = []
    factorial = 1.0
    for power in range(TERMS):
        factorial = factorial * (power + 1)
        series.append((end_time ** (power + 1) - start_time ** (power + 1)) / factorial)
    return jnp.stack(series)


def combine_terms(weights, taylor_terms):
    total = weights[0] * taylor_terms[0]
    for power in range(1, TERMS):
        total = total + weights[power] * taylor_terms[power]
    return total


def face_project(projection, values):
    face_modes = projection.shape[1]
    mode_count, quantity_count, element_count = values.shape
    result = jnp.dot(projection.reshape(4 * face_modes, mode_count), values.reshape(mode_count, quantity_count * element_count), precision=precise)
    return result.reshape(4, face_modes, quantity_count, element_count)


def end_update(integral, gathered, stiffness_op, projection, star_set, minus_set, plus_set):
    face_modes = projection.shape[1]
    mode_count, quantity_count, element_count = integral.shape
    own_traces = face_project(projection, integral)
    flux_terms = contract_small(gathered, plus_set[:, None]) - contract_small(own_traces, minus_set[:, None])
    lifted = jnp.dot(projection.reshape(4 * face_modes, mode_count).T, flux_terms.reshape(4 * face_modes, quantity_count * element_count), precision=precise)
    return apply_operator(integral, stiffness_op, star_set) + lifted.reshape(mode_count, quantity_count, element_count)


def materials(jacobians, minus_root, plus_flux, cluster_id):
    rate_values = jnp.where(cluster_id == 2, 4.0, jnp.where(cluster_id == 1, 2.0, 1.0)).astype(jacobians.dtype)
    star_set = rate_values * 0.5 * (jacobians + jnp.transpose(jacobians, (0, 2, 1, 3)))
    inner = minus_root.shape[2]
    product = minus_root[:, :, None, 0, :] * minus_root[:, None, :, 0, :]
    for index in range(1, inner):
        product = product + minus_root[:, :, None, index, :] * minus_root[:, None, :, index, :]
    minus_set = rate_values * product
    plus_set = rate_values * plus_flux
    period_steps = jnp.where(cluster_id == 2, 1, jnp.where(cluster_id == 1, 2, 4)).astype(jnp.int32)
    return star_set, minus_set, plus_set, period_steps


def reference(initial_dofs, jacobians, stiffness, projection, minus_root, plus_flux, cluster_id, neighbours, send_faces):
    device_total = N_GROUP * N_DEV
    mode_count, quantity_count, element_count = initial_dofs.shape
    face_modes = projection.shape[1]
    trace_width = face_modes * quantity_count
    stiffness_op = (stiffness - jnp.transpose(stiffness, (0, 2, 1))).reshape(3 * mode_count, mode_count)
    star_set, minus_set, plus_set, period_steps = materials(jacobians, minus_root, plus_flux, cluster_id)
    face_codes = neighbours[0].reshape(4, device_total, ELEM_DEV).transpose(1, 0, 2).reshape(device_total, 4 * ELEM_DEV)
    targets = send_faces.reshape(4, device_total, SLOTS).transpose(1, 0, 2).reshape(device_total, 4 * SLOTS)
    current = initial_dofs
    taylor_terms = jnp.zeros((TERMS, mode_count, quantity_count, element_count), initial_dofs.dtype)
    integral = jnp.zeros_like(initial_dofs)
    gathered = jnp.zeros((4, face_modes, quantity_count, element_count), initial_dofs.dtype)
    for substep in range(MACRO * 4):
        within = substep % 4
        starting = (within % period_steps) == 0
        ending = ((within + 1) % period_steps) == 0
        taylor_terms = jnp.where(starting, expansion(current, stiffness_op, star_set), taylor_terms)
        integral = jnp.where(starting, 0.0, integral)
        gathered = jnp.where(starting, 0.0, gathered)
        offsets = (within % period_steps).astype(initial_dofs.dtype)
        portion = combine_terms(coefficients(offsets), taylor_terms)
        integral = integral + portion
        traces = face_project(projection, portion)
        per_device = traces.reshape(4, face_modes, quantity_count, device_total, ELEM_DEV).transpose(3, 1, 2, 0, 4).reshape(device_total, trace_width, 4 * ELEM_DEV)
        outgoing = jax.vmap(lambda column_set, picked_ids: column_set[:, picked_ids])(per_device, targets)
        outgoing = outgoing.reshape(N_GROUP, N_DEV, trace_width, 4, SLOTS)
        blank_group = jnp.zeros_like(outgoing[:1, :, :, 0])
        blank_dev = jnp.zeros_like(outgoing[:, :1, :, 0])
        from_lower_group = jnp.concatenate([blank_group, outgoing[:-1, :, :, 1]], axis=0)
        from_upper_group = jnp.concatenate([outgoing[1:, :, :, 0], blank_group], axis=0)
        from_lower_dev = jnp.concatenate([blank_dev, outgoing[:, :-1, :, 3]], axis=1)
        from_upper_dev = jnp.concatenate([outgoing[:, 1:, :, 2], blank_dev], axis=1)
        incoming = jnp.stack([from_lower_group, from_upper_group, from_lower_dev, from_upper_dev], axis=3)
        incoming = incoming.reshape(device_total, trace_width, 4 * SLOTS)
        source = jnp.concatenate([per_device, incoming], axis=2)
        received = jax.vmap(lambda column_set, picked_ids: column_set[:, picked_ids])(source, face_codes)
        received = received.reshape(device_total, face_modes, quantity_count, 4, ELEM_DEV).transpose(3, 1, 2, 0, 4)
        gathered = gathered + received.reshape(4, face_modes, quantity_count, element_count)
        update = end_update(integral, gathered, stiffness_op, projection, star_set, minus_set, plus_set)
        current = jnp.where(ending, current + update, current)
    return current
```

```python
import functools
import math

import jax
import jax.numpy as jnp
from jax import lax
from jax.experimental import pallas as pl
from jax.experimental.pallas import tpu as pltpu
from jax.sharding import PartitionSpec as P

TERMS = 6
STEPS = 4
MESH = pl.DeviceIdType.MESH
f32, bf16 = jnp.float32, jnp.bfloat16

M, Q, E, FM = 56, 9, 32, 24
W = 384
K3 = 176
TR = 216


def weights(power, offset):
    start, end = offset * 0.25, offset * 0.25 + 0.25
    return (end ** (power + 1) - start ** (power + 1)) / math.factorial(power + 1)


def split(x):
    hi = x.astype(bf16)
    return hi, (x - hi.astype(f32)).astype(bf16)


def stacked(x):
    return jnp.concatenate(split(x), axis=0)


def dot3(stack, x):
    rows = stack.shape[0] // 2
    hi, lo = split(x)
    both = jnp.dot(stack, hi, preferred_element_type=f32)
    return both[:rows] + both[rows:] + jnp.dot(stack[:rows], lo, preferred_element_type=f32)


def lane_group(rows):
    return lax.broadcasted_iota(jnp.int32, (rows, 128), 1) // E


def spread(v):
    group = lane_group(v.shape[0])
    odd, high = (group % 2) == 1, group >= 2
    even = jnp.where(odd, pltpu.roll(v, 32, 1), v)
    other = jnp.where(odd, v, pltpu.roll(v, 96, 1))
    even_r, other_r = pltpu.roll(even, 64, 1), pltpu.roll(other, 64, 1)
    return (
        jnp.where(high, even_r, even),
        jnp.where(high, other_r, other),
        jnp.where(high, even, even_r),
        jnp.where(high, other, other_r),
    )


def star_product(x, star):
    parts = [[], [], []]
    for tile in range(M // 8):
        rows = x[tile * 8 : tile * 8 + 8]
        wide = (
            *spread(rows[:, :128]),
            *spread(rows[:, 128:256]),
            spread(rows[:, 256:])[0],
        )
        for d in range(3):
            lanes = []
            for t in range(3):
                cut = slice(t * 128, t * 128 + 128)
                total = wide[0] * star[d * Q, :, cut]
                for i in range(1, Q):
                    total = total + wide[i] * star[d * Q + i, :, cut]
                lanes.append(total)
            parts[d].append(jnp.concatenate(lanes, axis=1))
    pad = [jnp.zeros((K3 - 3 * M, W), f32)]
    return jnp.concatenate(parts[0] + parts[1] + parts[2] + pad, axis=0)


def operator(x, star, s_stack):
    return dot3(s_stack[...], star_product(x, star))[:M]


def to_face_lanes(t):
    group = lane_group(FM)
    out = []
    for q in range(Q):
        tile, g = q // 4, q % 4
        cut = slice(tile * 128, tile * 128 + 128)
        total = None
        for f in range(4):
            piece = t[f * FM : f * FM + FM, cut]
            piece = pltpu.roll(piece, (32 * (f - g)) % 128, 1) if f != g else piece
            total = piece if total is None else jnp.where(group == f, piece, total)
        out.append(total)
    return out


def to_quantity_lanes(flux):
    group = lane_group(FM)
    rows = []
    for f in range(4):
        lanes = []
        for t in range(3):
            total = jnp.zeros((FM, 128), f32)
            for j in range(4 * t, min(4 * t + 4, Q)):
                g = j % 4
                piece = pltpu.roll(flux[j], (32 * (g - f)) % 128, 1) if f != g else flux[j]
                total = jnp.where(group == g, piece, total)
            lanes.append(total)
        rows.append(jnp.concatenate(lanes, axis=1))
    return jnp.concatenate(rows, axis=0)


def contract(rows, table):
    out = []
    for j in range(Q):
        total = None
        for i in range(Q):
            left = rows[i].reshape(FM // 8, 8, 128)
            term = left * table[i * Q + j][None]
            total = term if total is None else total + term
        out.append(total.reshape(FM, 128))
    return out


def kernel(
    axes,
    dofs,
    jac,
    stiff,
    proj,
    root,
    plus_in,
    cluster,
    codes,
    out,
    star,
    minus,
    plus,
    s_stack,
    p_stack,
    pt_stack,
    p_rows,
    coef,
    mask,
    pick,
    owed,
    current,
    base,
    portion,
    pending,
    send_buf,
    recv_buf,
    send_sem,
    recv_sem,
):
    group, dev = lax.axis_index("group"), lax.axis_index("dev")
    n_group, n_dev = axes
    links = (
        (group > 0, {"group": group - 1}, 1),
        (group < n_group - 1, {"group": group + 1}, 0),
        (dev > 0, {"dev": dev - 1}, 3),
        (dev < n_dev - 1, {"dev": dev + 1}, 2),
    )
    send_buf[...] = jnp.zeros_like(send_buf)
    recv_buf[...] = jnp.zeros_like(recv_buf)
    barrier = pltpu.get_barrier_semaphore()
    for there, peer, _ in links:

        @pl.when(there)
        def _():
            pl.semaphore_signal(barrier, inc=1, device_id=peer, device_id_type=MESH)

    kind = cluster[...]
    rate = jnp.where(kind == 2, 4.0, jnp.where(kind == 1, 2.0, 1.0)).astype(f32)
    rate4 = jnp.concatenate([rate] * 4, axis=1)
    kind4 = jnp.concatenate([kind] * 4, axis=1)
    kind12 = jnp.broadcast_to(jnp.concatenate([kind4] * 3, axis=1), (8, W))
    for d in range(3):
        for i in range(Q):
            row = [
                0.5 * rate * (jac[i, j, d : d + 1, :] + jac[j, i, d : d + 1, :]) for j in range(Q)
            ]
            row = jnp.concatenate(row + [jnp.zeros((1, W - Q * E), f32)], axis=1)
            star[d * Q + i] = jnp.broadcast_to(row, (8, W))
    roots = []
    for i in range(Q):
        roots.append(jnp.concatenate([root[i, :, f, :] for f in range(4)], axis=1))
        row = jnp.concatenate([plus_in[i, :, f, :] for f in range(4)], axis=1) * rate4
        for j in range(Q):
            plus[i * Q + j] = jnp.broadcast_to(row[j : j + 1], (8, 128))
    for i in range(Q):
        for j in range(i, Q):
            row = jnp.sum(roots[i] * roots[j], axis=0, keepdims=True) * rate4
            row = jnp.broadcast_to(row, (8, 128))
            minus[i * Q + j] = row
            minus[j * Q + i] = row
    stiff_rows = [stiff[d] - jnp.transpose(stiff[d], (1, 0)) for d in range(3)]
    stiff_rows = jnp.concatenate(stiff_rows + [jnp.zeros((M, K3 - 3 * M), f32)], axis=1)
    s_stack[...] = stacked(jnp.concatenate([stiff_rows, jnp.zeros((8, K3), f32)], axis=0))
    p_rows[...] = jnp.zeros_like(p_rows)
    for f in range(4):
        p_rows[f * FM : f * FM + 21, 0:M] = proj[:, f, :]
    p_stack[...] = stacked(p_rows[...])
    pt_stack[...] = stacked(jnp.transpose(p_rows[...], (1, 0)))
    for u in range(STEPS):
        first = [kind12 == 2, kind12 == 1]
        starting = (True, first[0], first[0] | first[1], first[0])[u]
        mask[u] = jnp.ones((8, W), f32) if u == 0 else jnp.where(starting, 1.0, 0.0).astype(f32)
        for k in range(TERMS):
            coef[u * TERMS + k] = jnp.where(
                first[0],
                weights(k, 0),
                jnp.where(first[1], weights(k, u % 2), weights(k, u)),
            ).astype(f32)
    mask[STEPS] = jnp.ones((8, W), f32)
    code = jnp.concatenate([codes[0, f : f + 1, :] for f in range(4)], axis=1)
    local = lax.broadcasted_iota(jnp.int32, (128, 128), 0) == code
    local = jnp.where(local, 1.0, 0.0).astype(f32).astype(bf16)
    pick[...] = jnp.concatenate([local, local], axis=0)
    remote = lax.broadcasted_iota(jnp.int32, (32, 128), 0) + 128 == code
    remote = jnp.where(remote, 1.0, 0.0).astype(f32).astype(bf16)
    owed[...] = jnp.concatenate([remote, remote], axis=1)
    current[...] = jnp.zeros_like(current)
    current[:, 0 : Q * E] = jnp.transpose(dofs[...].reshape(Q * E, M), (1, 0))
    base[...] = jnp.zeros_like(base)
    pending[...] = jnp.zeros_like(pending)

    def tall(row):
        return jnp.broadcast_to(row[None], (M // 8, 8, W)).reshape(M, W)

    def exchange(u, p):
        there, peer, back = links[p]
        return pltpu.make_async_remote_copy(
            src_ref=send_buf.at[u, p],
            dst_ref=recv_buf.at[u, back],
            send_sem=send_sem.at[u, p],
            recv_sem=recv_sem.at[u, back],
            device_id=peer,
            device_id_type=MESH,
        )

    def landed(u, p):
        there, peer, _ = links[p]
        return pltpu.make_async_remote_copy(
            src_ref=send_buf.at[u, p],
            dst_ref=recv_buf.at[u, p],
            send_sem=send_sem.at[u, p],
            recv_sem=recv_sem.at[u, p],
            device_id=peer,
            device_id_type=MESH,
        )

    def substep(u, first):
        starting = tall(mask[u]) > 0.5
        x = jnp.where(starting, current[...], base[...])
        base[...] = x

        def term(k, carry):
            x, total = carry
            x = operator(x, star, s_stack)
            return x, total + tall(coef[u * TERMS + k]) * x

        x, total = lax.fori_loop(1, TERMS, term, (x, tall(coef[u * TERMS]) * x))
        portion[...] = total
        padded = jnp.concatenate([total, jnp.zeros((8, W), f32)], axis=0)
        traces = to_face_lanes(dot3(p_stack[...], padded))
        both = jnp.concatenate(
            split(jnp.concatenate(traces + [jnp.zeros((8, 128), f32)], axis=0)), axis=1
        )
        outgoing = lax.dot_general(
            owed[...], both, (((1,), (1,)), ((), ())), preferred_element_type=f32
        )
        for p in range(4):
            send_buf[u, p, :, 0:224] = outgoing[p * 8 : p * 8 + 8]
        if first:
            pl.semaphore_wait(barrier, sum(there.astype(jnp.int32) for there, _, _ in links))

        for p in (3, 2, 0, 1):

            @pl.when(links[p][0])
            def _():
                exchange(u, p).start()

        taken = jnp.dot(both, pick[...], preferred_element_type=f32)
        taken = [taken[q * FM : q * FM + FM] for q in range(Q)]
        own = contract(traces, minus)
        flux = [a - b for a, b in zip(contract(taken, plus), own)]
        pending[...] = (
            jnp.where(starting, 0.0, pending[...])
            + operator(portion[...], star, s_stack)
            + dot3(pt_stack[...], to_quantity_lanes(flux))[:M]
        )
        for p in (0, 1, 2, 3):

            @pl.when(links[p][0])
            def _():
                exchange(u, p).wait_send()
                landed(u, p).wait_recv()

        arrived = recv_buf[u].reshape(32, 256)
        arrived = jnp.transpose(arrived, (1, 0))[:224]
        hi, lo = split(arrived)
        spot = owed[:, 0:128]
        taken = jnp.dot(hi, spot, preferred_element_type=f32) + jnp.dot(
            lo, spot, preferred_element_type=f32
        )
        taken = [taken[q * FM : q * FM + FM] for q in range(Q)]
        flux = contract(taken, plus)
        total = pending[...] + dot3(pt_stack[...], to_quantity_lanes(flux))[:M]
        pending[...] = total
        ending = tall(mask[u + 1]) > 0.5
        current[...] = jnp.where(ending, current[...] + total, current[...])

    substep(0, True)

    def later(u, _):
        substep(u, False)
        return 0

    lax.fori_loop(1, STEPS, later, 0)
    out[...] = jnp.transpose(current[:, 0 : Q * E], (1, 0)).reshape(Q, E, M)


def on_device(dofs, jac, stiff, proj, root, plus_in, cluster, codes, send_faces):
    axes = (lax.axis_size("group"), lax.axis_size("dev"))
    scratch = [
        pltpu.VMEM((27, 8, W), f32),
        pltpu.VMEM((81, 8, 128), f32),
        pltpu.VMEM((81, 8, 128), f32),
        pltpu.VMEM((128, K3), bf16),
        pltpu.VMEM((8 * FM, 64), bf16),
        pltpu.VMEM((128, 4 * FM), bf16),
        pltpu.VMEM((4 * FM, 64), f32),
        pltpu.VMEM((STEPS * TERMS, 8, W), f32),
        pltpu.VMEM((STEPS + 1, 8, W), f32),
        pltpu.VMEM((256, 128), bf16),
        pltpu.VMEM((32, 256), bf16),
        pltpu.VMEM((M, W), f32),
        pltpu.VMEM((M, W), f32),
        pltpu.VMEM((M, W), f32),
        pltpu.VMEM((M, W), f32),
        pltpu.VMEM((STEPS, 4, 8, 256), f32),
        pltpu.VMEM((STEPS, 4, 8, 256), f32),
        pltpu.SemaphoreType.DMA((STEPS, 4)),
        pltpu.SemaphoreType.DMA((STEPS, 4)),
    ]
    final = pl.pallas_call(
        functools.partial(kernel, axes),
        out_shape=jax.ShapeDtypeStruct((Q, E, M), f32),
        in_specs=[pl.BlockSpec(memory_space=pltpu.VMEM)] * 8,
        out_specs=pl.BlockSpec(memory_space=pltpu.VMEM),
        scratch_shapes=scratch,
        compiler_params=pltpu.CompilerParams(collective_id=0, has_side_effects=True),
        name="lts_update",
    )(
        jnp.transpose(dofs, (1, 2, 0)),
        jnp.transpose(jac, (1, 2, 0, 3)),
        stiff,
        jnp.transpose(proj, (1, 0, 2)),
        jnp.transpose(root, (1, 2, 0, 3)),
        jnp.transpose(plus_in, (1, 2, 0, 3)),
        cluster.reshape(1, E),
        codes,
    )
    return jnp.transpose(final, (2, 0, 1))


def solution(mesh):
    placed = (
        P(None, None, ("group", "dev")),
        P(None, None, None, ("group", "dev")),
        P(),
        P(),
        P(None, None, None, ("group", "dev")),
        P(None, None, None, ("group", "dev")),
        P(("group", "dev")),
        P(None, None, ("group", "dev")),
        P(None, ("group", "dev")),
    )
    return jax.shard_map(
        on_device,
        mesh=mesh,
        in_specs=placed,
        out_specs=P(None, None, ("group", "dev")),
        check_vma=False,
    )
```

```python
import functools
import math

import jax
import jax.numpy as jnp
from jax import lax
from jax.experimental import pallas as pl
from jax.experimental.pallas import tpu as pltpu
from jax.sharding import PartitionSpec as P

TERMS = 6
STEPS = 4
MESH = pl.DeviceIdType.MESH
f32, bf16 = jnp.float32, jnp.bfloat16

M, Q, E, FM = 56, 9, 32, 24
W = 384
K3 = 176
TR = 216


def weights(power, offset):
    start, end = offset * 0.25, offset * 0.25 + 0.25
    return (end ** (power + 1) - start ** (power + 1)) / math.factorial(power + 1)


def split(x):
    hi = x.astype(bf16)
    return hi, (x - hi.astype(f32)).astype(bf16)


def stacked(x):
    return jnp.concatenate(split(x), axis=0)


def dot3(stack, x):
    rows = stack.shape[0] // 2
    hi, lo = split(x)
    both = jnp.dot(stack, hi, preferred_element_type=f32)
    return both[:rows] + both[rows:] + jnp.dot(stack[:rows], lo, preferred_element_type=f32)


def lane_group(rows):
    return lax.broadcasted_iota(jnp.int32, (rows, 128), 1) // E


def spread(v):
    group = lane_group(v.shape[0])
    odd, high = (group % 2) == 1, group >= 2
    even = jnp.where(odd, pltpu.roll(v, 32, 1), v)
    other = jnp.where(odd, v, pltpu.roll(v, 96, 1))
    even_r, other_r = pltpu.roll(even, 64, 1), pltpu.roll(other, 64, 1)
    return (
        jnp.where(high, even_r, even),
        jnp.where(high, other_r, other),
        jnp.where(high, even, even_r),
        jnp.where(high, other, other_r),
    )


def star_product(x, star):
    parts = [[], [], []]
    for tile in range(M // 8):
        rows = x[tile * 8 : tile * 8 + 8]
        wide = (
            *spread(rows[:, :128]),
            *spread(rows[:, 128:256]),
            spread(rows[:, 256:])[0],
        )
        for d in range(3):
            lanes = []
            for t in range(3):
                cut = slice(t * 128, t * 128 + 128)
                total = wide[0] * star[d * Q, :, cut]
                for i in range(1, Q):
                    total = total + wide[i] * star[d * Q + i, :, cut]
                lanes.append(total)
            parts[d].append(jnp.concatenate(lanes, axis=1))
    pad = [jnp.zeros((K3 - 3 * M, W), f32)]
    return jnp.concatenate(parts[0] + parts[1] + parts[2] + pad, axis=0)


def operator(x, star, s_stack):
    return dot3(s_stack[...], star_product(x, star))[:M]


def to_face_lanes(t):
    group = lane_group(FM)
    out = []
    for q in range(Q):
        tile, g = q // 4, q % 4
        cut = slice(tile * 128, tile * 128 + 128)
        total = None
        for f in range(4):
            piece = t[f * FM : f * FM + FM, cut]
            piece = pltpu.roll(piece, (32 * (f - g)) % 128, 1) if f != g else piece
            total = piece if total is None else jnp.where(group == f, piece, total)
        out.append(total)
    return out


def to_quantity_lanes(flux):
    group = lane_group(FM)
    rows = []
    for f in range(4):
        lanes = []
        for t in range(3):
            total = jnp.zeros((FM, 128), f32)
            for j in range(4 * t, min(4 * t + 4, Q)):
                g = j % 4
                piece = pltpu.roll(flux[j], (32 * (g - f)) % 128, 1) if f != g else flux[j]
                total = jnp.where(group == g, piece, total)
            lanes.append(total)
        rows.append(jnp.concatenate(lanes, axis=1))
    return jnp.concatenate(rows, axis=0)


def contract(rows, table):
    out = []
    for j in range(Q):
        total = None
        for i in range(Q):
            left = rows[i].reshape(FM // 8, 8, 128)
            term = left * table[i * Q + j][None]
            total = term if total is None else total + term
        out.append(total.reshape(FM, 128))
    return out


def kernel(
    axes,
    dofs,
    jac,
    stiff,
    proj,
    root,
    plus_in,
    cluster,
    codes,
    out,
    star,
    minus,
    plus,
    s_stack,
    p_stack,
    pt_stack,
    p_rows,
    coef,
    mask,
    pick,
    owed,
    base,
    portion,
    pending,
    inbox,
    send_buf,
    recv_buf,
    fixed_send,
    fixed_recv,
    far_star,
    far_plus,
    far_place,
    answer,
    send_sem,
    recv_sem,
    fixed_sem,
):
    group, dev = lax.axis_index("group"), lax.axis_index("dev")
    n_group, n_dev = axes
    half = n_dev // 2
    links = (
        (group > 0, {"group": group - 1}, 1),
        (group < n_group - 1, {"group": group + 1}, 0),
        (dev > 0, {"dev": dev - 1}, 3),
        (dev < n_dev - 1, {"dev": dev + 1}, 2),
    )
    far = {2: dev == half, 3: dev == half - 1}
    is_far = (dev == half) | (dev == half - 1)
    near = [links[0][0], links[1][0], (dev > 0) & (dev != half)]
    near.append((dev < n_dev - 1) & (dev != half - 1))
    barrier = pltpu.get_barrier_semaphore()
    for there, peer, _ in links:

        @pl.when(there)
        def _():
            pl.semaphore_signal(barrier, inc=1, device_id=peer, device_id_type=MESH)

    send_buf[...] = jnp.zeros_like(send_buf)

    kind = cluster[...]
    rate = jnp.where(kind == 2, 4.0, jnp.where(kind == 1, 2.0, 1.0)).astype(f32)
    rate4 = jnp.concatenate([rate] * 4, axis=1)
    kind4 = jnp.concatenate([kind] * 4, axis=1)
    kind12 = jnp.broadcast_to(jnp.concatenate([kind4] * 3, axis=1), (8, W))
    for d in range(3):
        for i in range(Q):
            row = [
                0.5 * rate * (jac[i, j, d : d + 1, :] + jac[j, i, d : d + 1, :]) for j in range(Q)
            ]
            row = jnp.concatenate(row + [jnp.zeros((1, W - Q * E), f32)], axis=1)
            star[d * Q + i] = jnp.broadcast_to(row, (8, W))
    roots = []
    for i in range(Q):
        roots.append(jnp.concatenate([root[i, :, f, :] for f in range(4)], axis=1))
        row = jnp.concatenate([plus_in[i, :, f, :] for f in range(4)], axis=1) * rate4
        for j in range(Q):
            plus[i * Q + j] = jnp.broadcast_to(row[j : j + 1], (8, 128))
    for i in range(Q):
        for j in range(i, Q):
            row = jnp.sum(roots[i] * roots[j], axis=0, keepdims=True) * rate4
            row = jnp.broadcast_to(row, (8, 128))
            minus[i * Q + j] = row
            minus[j * Q + i] = row
    stiff_rows = [stiff[d] - jnp.transpose(stiff[d], (1, 0)) for d in range(3)]
    stiff_rows = jnp.concatenate(stiff_rows + [jnp.zeros((M, K3 - 3 * M), f32)], axis=1)
    s_stack[...] = stacked(jnp.concatenate([stiff_rows, jnp.zeros((8, K3), f32)], axis=0))
    p_rows[...] = jnp.zeros_like(p_rows)
    for f in range(4):
        p_rows[f * FM : f * FM + 21, 0:M] = proj[:, f, :]
    p_stack[...] = stacked(p_rows[...])
    pt_stack[...] = stacked(jnp.transpose(p_rows[...], (1, 0)))
    for u in range(STEPS):
        first = [kind12 == 2, kind12 == 1]
        starting = (True, first[0], first[0] | first[1], first[0])[u]
        mask[u] = jnp.ones((8, W), f32) if u == 0 else jnp.where(starting, 1.0, 0.0).astype(f32)
        for k in range(TERMS):
            coef[u * TERMS + k] = jnp.where(
                first[0],
                weights(k, 0),
                jnp.where(first[1], weights(k, u % 2), weights(k, u)),
            ).astype(f32)
    code = jnp.concatenate([codes[0, f : f + 1, :] for f in range(4)], axis=1)
    local = lax.broadcasted_iota(jnp.int32, (128, 128), 0) == code
    local = jnp.where(local, 1.0, 0.0).astype(f32).astype(bf16)
    pick[...] = jnp.concatenate([local, local], axis=0)
    remote = lax.broadcasted_iota(jnp.int32, (32, 128), 0) + 128 == code
    remote = jnp.where(remote, 1.0, 0.0).astype(f32).astype(bf16)
    owed[...] = jnp.concatenate([remote, remote], axis=1)
    base[...] = jnp.zeros_like(base)
    base[:, 0 : Q * E] = jnp.transpose(dofs[...].reshape(Q * E, M), (1, 0))
    pending[...] = jnp.zeros_like(pending)

    def tall(row):
        return jnp.broadcast_to(row[None], (M // 8, 8, W)).reshape(M, W)

    def exchange(u, p, slot):
        return pltpu.make_async_remote_copy(
            src_ref=send_buf.at[u, p],
            dst_ref=recv_buf.at[u, slot],
            send_sem=send_sem.at[u, p],
            recv_sem=recv_sem.at[u, slot],
            device_id=links[p][1],
            device_id_type=MESH,
        )

    def send(u, p):
        exchange(u, p, links[p][2]).start()

    def collect(u, p):
        exchange(u, p, links[p][2]).wait_send()
        exchange(u, p, p).wait_recv()

    def fixed(p):
        return pltpu.make_async_remote_copy(
            src_ref=fixed_send,
            dst_ref=fixed_recv,
            send_sem=fixed_sem.at[0],
            recv_sem=fixed_sem.at[1],
            device_id=links[p][1],
            device_id_type=MESH,
        )

    def expand(u, x, table):
        def term(k, carry):
            x, total = carry
            x = operator(x, table, s_stack)
            return x, total + tall(coef[u * TERMS + k]) * x

        return lax.fori_loop(1, TERMS, term, (x, tall(coef[u * TERMS]) * x))[1]

    def project(total):
        padded = jnp.concatenate([total, jnp.zeros((8, W), f32)], axis=0)
        traces = to_face_lanes(dot3(p_stack[...], padded))
        rows = jnp.concatenate(traces + [jnp.zeros((8, 128), f32)], axis=0)
        return traces, jnp.concatenate(split(rows), axis=1)

    def rows_for(places, both):
        return lax.dot_general(
            places, both, (((1,), (1,)), ((), ())), preferred_element_type=f32
        )

    def lifted(flux):
        return dot3(pt_stack[...], to_quantity_lanes(flux))[:M]

    def placed(rows, places, count):
        hi, lo = split(jnp.transpose(rows, (1, 0))[:count])
        return jnp.dot(hi, places, preferred_element_type=f32) + jnp.dot(
            lo, places, preferred_element_type=f32
        )

    def received(rows, places, table):
        taken = placed(rows, places, 224)
        return lifted(contract([taken[q * FM : q * FM + FM] for q in range(Q)], table))

    def absorb():
        pending[...] += received(inbox[...], owed[:, 0:128], plus)

    def stay(u, traces, both):
        taken = jnp.dot(both, pick[...], preferred_element_type=f32)
        taken = [taken[q * FM : q * FM + FM] for q in range(Q)]
        flux = [a - b for a, b in zip(contract(taken, plus), contract(traces, minus))]
        pending[...] = (
            jnp.where(tall(mask[u]) > 0.5, 0.0, pending[...])
            + operator(portion[...], star, s_stack)
            + lifted(flux)
        )

    def pack_fixed():
        for p, there in far.items():

            @pl.when(there)
            def _():
                v = owed[:, 0:128].astype(f32)[p * 8 : p * 8 + 8]
                v = v + pltpu.roll(v, 64, 1)
                v = v + pltpu.roll(v, 32, 1)
                v = jnp.concatenate([v] * 3, axis=1)
                lane = lax.broadcasted_iota(jnp.int32, (8, W), 1) // E
                chosen = [jnp.where(lane == j, v, 0.0) for j in range(Q)]
                chosen = jnp.concatenate(chosen + [jnp.zeros((56, W), f32)], axis=0).astype(bf16)
                rows = jnp.concatenate([star[:, 0, :], jnp.zeros((5, W), f32)], axis=0)
                hi, lo = split(rows)
                fixed_send[0:32] = rows_for(hi, chosen) + rows_for(lo, chosen)
                lane = lax.broadcasted_iota(jnp.int32, (1, 128), 1)
                fast = jnp.where(kind4 == 2, 1.0, 0.0).astype(f32)
                rows = jnp.concatenate(
                    [
                        plus[:, 0, :] * fast,
                        (lane % E).astype(f32),
                        (lane // E).astype(f32),
                        jnp.zeros((45, 128), f32),
                    ],
                    axis=0,
                )
                rows = rows_for(owed[...], jnp.concatenate(split(rows), axis=1))
                fixed_send[32:40] = rows[p * 8 : p * 8 + 8]

    def unpack_fixed():
        for p, there in far.items():

            @pl.when(there)
            def _():
                fixed(p).wait_send()
                fixed(p).wait_recv()
                row = lax.broadcasted_iota(jnp.int32, (128, W), 0)
                lane = lax.broadcasted_iota(jnp.int32, (128, W), 1)
                wide = (lane // E == row // 8) & (lane % E == p * 8 + row % 8)
                wide = jnp.where(wide, 1.0, 0.0).astype(f32).astype(bf16)
                hi, lo = split(fixed_recv[0:32])
                rows = jnp.dot(hi, wide, preferred_element_type=f32)
                rows = rows + jnp.dot(lo, wide, preferred_element_type=f32)
                for r in range(27):
                    far_star[r] = jnp.broadcast_to(rows[r : r + 1], (8, W))
                rows = fixed_recv[32:40]
                lane = lax.broadcasted_iota(jnp.int32, (8, 128), 1).astype(f32)
                element, face = rows[:, 81:82], rows[:, 82:83]
                owner = jnp.where(lane == element, 1.0, 0.0).astype(f32).astype(bf16)
                same = rows_for(owner, owner)
                order = lax.broadcasted_iota(jnp.int32, (8, 8), 1).astype(f32)
                leader = jnp.min(jnp.where(same > 0.5, order, 8.0), axis=1, keepdims=True)
                spot = jnp.where(lane == face * E + (p * 8) + leader, 1.0, 0.0).astype(f32)
                blank = [jnp.zeros((8, 128), f32)]
                spots = jnp.concatenate(blank * p + [spot] + blank * (3 - p), axis=0).astype(bf16)
                far_place[...] = jnp.concatenate([spots, spots], axis=1)
                rows = jnp.concatenate(blank * p + [rows] + blank * (3 - p), axis=0)
                rows = placed(rows, spots, 88)
                for r in range(81):
                    far_plus[r] = jnp.broadcast_to(rows[r : r + 1], (8, 128))

    def pair(h, _):
        u, v = 2 * h, 2 * h + 1
        total = expand(u, base[...], star)
        portion[...] = total
        traces, both = project(total)
        outgoing = rows_for(owed[...], both)
        for p in range(4):
            send_buf[u, p, :, 0:224] = outgoing[p * 8 : p * 8 + 8]

        @pl.when(h == 0)
        def _():
            pack_fixed()
            pl.semaphore_wait(barrier, sum(there.astype(jnp.int32) for there, _, _ in links))

        for p in (3, 2, 0, 1):

            @pl.when(links[p][0])
            def _():
                send(u, p)

        for p, there in far.items():

            @pl.when(there & (h == 0))
            def _():
                fixed(p).start()

        stay(u, traces, both)
        inbox[...] = jnp.zeros_like(inbox)
        for p in range(4):

            @pl.when(near[p])
            def _():
                collect(u, p)
                inbox[p * 8 : p * 8 + 8] = recv_buf[u, p]

        absorb()

        @pl.when(is_far)
        def _():
            x = jnp.where(tall(mask[v]) > 0.5, base[...] + pending[...], base[...])
            early = rows_for(owed[...], project(expand(v, x, star))[1])
            for p, there in far.items():

                @pl.when(there)
                def _():
                    send_buf[v, p, :, 0:224] = early[p * 8 : p * 8 + 8]
                    send(v, p)

            inbox[...] = jnp.zeros_like(inbox)
            for p, there in far.items():

                @pl.when(there)
                def _():
                    collect(u, p)
                    inbox[p * 8 : p * 8 + 8] = recv_buf[u, p]

            absorb()

        x = jnp.where(tall(mask[v]) > 0.5, base[...] + pending[...], base[...])
        base[...] = x
        total = expand(v, x, star)
        portion[...] = total
        traces, both = project(total)
        outgoing = rows_for(owed[...], both)
        for p in range(4):

            @pl.when(near[p])
            def _():
                send_buf[v, p, :, 0:224] = outgoing[p * 8 : p * 8 + 8]
                send(v, p)

        stay(v, traces, both)
        inbox[...] = jnp.zeros_like(inbox)

        @pl.when(is_far)
        def _():
            @pl.when(h == 0)
            def _():
                unpack_fixed()

            mine = send_buf[u].reshape(32, 256)
            x = received(mine, far_place[:, 0:128], far_plus)
            both = project(expand(0, x, far_star))[1]
            answer[:, 0:224] = rows_for(far_place[...], both)
            for p, there in far.items():

                @pl.when(there)
                def _():
                    collect(v, p)
                    rows = slice(p * 8, p * 8 + 8)
                    inbox[rows, 0:224] = recv_buf[v, p, :, 0:224] + answer[rows, 0:224]

        for p in range(4):

            @pl.when(near[p])
            def _():
                collect(v, p)
                inbox[p * 8 : p * 8 + 8] = recv_buf[v, p]

        absorb()
        last = h == STEPS // 2 - 1
        following = jnp.minimum(v + 1, STEPS - 1)
        ending = (tall(mask[following]) > 0.5) | last
        base[...] = jnp.where(ending, base[...] + pending[...], base[...])
        return 0

    lax.fori_loop(0, STEPS // 2, pair, 0)
    out[...] = jnp.transpose(base[:, 0 : Q * E], (1, 0)).reshape(Q, E, M)


def on_device(dofs, jac, stiff, proj, root, plus_in, cluster, codes, send_faces):
    axes = (lax.axis_size("group"), lax.axis_size("dev"))
    scratch = [
        pltpu.VMEM((27, 8, W), f32),
        pltpu.VMEM((81, 8, 128), f32),
        pltpu.VMEM((81, 8, 128), f32),
        pltpu.VMEM((128, K3), bf16),
        pltpu.VMEM((8 * FM, 64), bf16),
        pltpu.VMEM((128, 4 * FM), bf16),
        pltpu.VMEM((4 * FM, 64), f32),
        pltpu.VMEM((STEPS * TERMS, 8, W), f32),
        pltpu.VMEM((STEPS, 8, W), f32),
        pltpu.VMEM((256, 128), bf16),
        pltpu.VMEM((32, 256), bf16),
        pltpu.VMEM((M, W), f32),
        pltpu.VMEM((M, W), f32),
        pltpu.VMEM((M, W), f32),
        pltpu.VMEM((32, 256), f32),
        pltpu.VMEM((STEPS, 4, 8, 256), f32),
        pltpu.VMEM((STEPS, 4, 8, 256), f32),
        pltpu.VMEM((40, 128), f32),
        pltpu.VMEM((40, 128), f32),
        pltpu.VMEM((27, 8, W), f32),
        pltpu.VMEM((81, 8, 128), f32),
        pltpu.VMEM((32, 256), bf16),
        pltpu.VMEM((32, 256), f32),
        pltpu.SemaphoreType.DMA((STEPS, 4)),
        pltpu.SemaphoreType.DMA((STEPS, 4)),
        pltpu.SemaphoreType.DMA((2,)),
    ]
    final = pl.pallas_call(
        functools.partial(kernel, axes),
        out_shape=jax.ShapeDtypeStruct((Q, E, M), f32),
        in_specs=[pl.BlockSpec(memory_space=pltpu.VMEM)] * 8,
        out_specs=pl.BlockSpec(memory_space=pltpu.VMEM),
        scratch_shapes=scratch,
        compiler_params=pltpu.CompilerParams(collective_id=0, has_side_effects=True),
        name="lts_update",
    )(
        jnp.transpose(dofs, (1, 2, 0)),
        jnp.transpose(jac, (1, 2, 0, 3)),
        stiff,
        jnp.transpose(proj, (1, 0, 2)),
        jnp.transpose(root, (1, 2, 0, 3)),
        jnp.transpose(plus_in, (1, 2, 0, 3)),
        cluster.reshape(1, E),
        codes,
    )
    return jnp.transpose(final, (2, 0, 1))


def solution(mesh):
    placed = (
        P(None, None, ("group", "dev")),
        P(None, None, None, ("group", "dev")),
        P(),
        P(),
        P(None, None, None, ("group", "dev")),
        P(None, None, None, ("group", "dev")),
        P(("group", "dev")),
        P(None, None, ("group", "dev")),
        P(None, ("group", "dev")),
    )
    return jax.shard_map(
        on_device,
        mesh=mesh,
        in_specs=placed,
        out_specs=P(None, None, ("group", "dev")),
        check_vma=False,
    )
```

```python
import functools
import math

import jax
import jax.numpy as jnp
from jax import lax
from jax.experimental import pallas as pl
from jax.experimental.pallas import tpu as pltpu
from jax.sharding import PartitionSpec as P

TERMS = 6
STEPS = 4
MESH = pl.DeviceIdType.MESH
f32, bf16 = jnp.float32, jnp.bfloat16

M, Q, E, FM = 56, 9, 32, 24
W = 384
K3 = 176
TR = 216


def weights(power, offset):
    start, end = offset * 0.25, offset * 0.25 + 0.25
    return (end ** (power + 1) - start ** (power + 1)) / math.factorial(power + 1)


def split(x):
    hi = x.astype(bf16)
    return hi, (x - hi.astype(f32)).astype(bf16)


def stacked(x):
    return jnp.concatenate(split(x), axis=0)


def dot3(stack, x):
    rows = stack.shape[0] // 2
    hi, lo = split(x)
    both = jnp.dot(stack, hi, preferred_element_type=f32)
    return both[:rows] + both[rows:] + jnp.dot(stack[:rows], lo, preferred_element_type=f32)


def lane_group(rows):
    return lax.broadcasted_iota(jnp.int32, (rows, 128), 1) // E


def spread(v):
    group = lane_group(v.shape[0])
    odd, high = (group % 2) == 1, group >= 2
    even = jnp.where(odd, pltpu.roll(v, 32, 1), v)
    other = jnp.where(odd, v, pltpu.roll(v, 96, 1))
    even_r, other_r = pltpu.roll(even, 64, 1), pltpu.roll(other, 64, 1)
    return (
        jnp.where(high, even_r, even),
        jnp.where(high, other_r, other),
        jnp.where(high, even, even_r),
        jnp.where(high, other, other_r),
    )


def quad(stack, y):
    rows = stack.shape[0] // 2
    both = jnp.dot(stack, jnp.concatenate(split(y), axis=1), preferred_element_type=f32)
    return (both[:rows, :128] + both[rows:, :128]) + (both[:rows, 128:] + both[rows:, 128:])


def operator(x, star, s_stack):
    tiles = M // 8
    wide = []
    for tile in range(tiles):
        rows = x[tile * 8 : tile * 8 + 8]
        wide.append(
            (*spread(rows[:, :128]), *spread(rows[:, 128:256]), spread(rows[:, 256:])[0])
        )

    def weighted(tile, at):
        total = wide[tile][0] * star[at]
        for i in range(1, Q):
            total = total + wide[tile][i] * star[i * 7 + at]
        return total

    blank = [jnp.zeros((8, 128), f32)]
    last = [weighted(tile, 6) for tile in range(tiles)]
    rolled = [pltpu.roll(y, 96, 1) for y in last] + [pltpu.roll(y, 64, 1) for y in last]
    stack = s_stack[...]
    out = [quad(stack, jnp.concatenate(last + rolled + blank, axis=0))]
    for t in range(2):
        y = [weighted(tile, d * 2 + t) for d in range(3) for tile in range(tiles)]
        out.append(quad(stack, jnp.concatenate(y + blank, axis=0)))
    return jnp.concatenate([out[1][:M], out[2][:M], out[0][:M]], axis=1)


def to_face_lanes(t):
    group = lane_group(FM)
    out = []
    for q in range(Q):
        tile, g = q // 4, q % 4
        cut = slice(tile * 128, tile * 128 + 128)
        total = None
        for f in range(4):
            piece = t[f * FM : f * FM + FM, cut]
            piece = pltpu.roll(piece, (32 * (f - g)) % 128, 1) if f != g else piece
            total = piece if total is None else jnp.where(group == f, piece, total)
        out.append(total)
    return out


def to_quantity_lanes(flux):
    group = lane_group(FM)
    rows = []
    for f in range(4):
        lanes = []
        for t in range(3):
            total = jnp.zeros((FM, 128), f32)
            for j in range(4 * t, min(4 * t + 4, Q)):
                g = j % 4
                piece = pltpu.roll(flux[j], (32 * (g - f)) % 128, 1) if f != g else flux[j]
                total = jnp.where(group == g, piece, total)
            lanes.append(total)
        rows.append(jnp.concatenate(lanes, axis=1))
    return jnp.concatenate(rows, axis=0)


def contract(rows, table):
    out = []
    for j in range(Q):
        total = None
        for i in range(Q):
            left = rows[i].reshape(FM // 8, 8, 128)
            term = left * table[i * Q + j][None]
            total = term if total is None else total + term
        out.append(total.reshape(FM, 128))
    return out


def kernel(
    axes,
    *refs,
):
    inputs, (out, *refs) = refs[:8], refs[8:]
    held, copy_sem, refs = refs[:8], refs[8], refs[9:]
    copies = [pltpu.make_async_copy(a, b, copy_sem.at[i]) for i, (a, b) in enumerate(zip(inputs, held))]
    body(axes, copies, *held, out, *refs)


def body(
    axes,
    copies,
    dofs,
    jac,
    stiff,
    proj,
    root,
    plus_in,
    cluster,
    codes,
    out,
    star,
    minus,
    plus,
    s_stack,
    p_stack,
    pt_stack,
    p_rows,
    coef,
    mask,
    pick,
    owed,
    base,
    portion,
    pending,
    inbox,
    send_buf,
    recv_buf,
    fixed_send,
    fixed_recv,
    far_star,
    far_plus,
    far_place,
    answer,
    send_sem,
    recv_sem,
    fixed_sem,
):
    group, dev = lax.axis_index("group"), lax.axis_index("dev")
    n_group, n_dev = axes
    half = n_dev // 2
    links = (
        (group > 0, {"group": group - 1}, 1),
        (group < n_group - 1, {"group": group + 1}, 0),
        (dev > 0, {"dev": dev - 1}, 3),
        (dev < n_dev - 1, {"dev": dev + 1}, 2),
    )
    far = {2: dev == half, 3: dev == half - 1}
    is_far = (dev == half) | (dev == half - 1)
    near = [links[0][0], links[1][0], (dev > 0) & (dev != half)]
    near.append((dev < n_dev - 1) & (dev != half - 1))
    barrier = pltpu.get_barrier_semaphore()
    for there, peer, _ in links:

        @pl.when(there)
        def _():
            pl.semaphore_signal(barrier, inc=1, device_id=peer, device_id_type=MESH)

    for copy in copies:
        copy.start()
    send_buf[...] = jnp.zeros_like(send_buf)
    fixed_send[...] = jnp.zeros_like(fixed_send)

    for copy in copies:
        copy.wait()

    kind = cluster[...]
    rate = jnp.where(kind == 2, 4.0, jnp.where(kind == 1, 2.0, 1.0)).astype(f32)
    rate4 = jnp.concatenate([rate] * 4, axis=1)
    kind4 = jnp.concatenate([kind] * 4, axis=1)
    kind12 = jnp.broadcast_to(jnp.concatenate([kind4] * 3, axis=1), (8, W))
    last = [[] for _ in range(Q)]
    for d in range(3):
        for i in range(Q):
            row = [
                0.5 * rate * (jac[i, j, d : d + 1, :] + jac[j, i, d : d + 1, :]) for j in range(Q)
            ]
            last[i].append(row[8])
            for t in range(2):
                tile = jnp.concatenate(row[4 * t : 4 * t + 4], axis=1)
                star[i * 7 + d * 2 + t] = jnp.broadcast_to(tile, (8, 128))
    for i in range(Q):
        tile = jnp.concatenate(last[i] + [jnp.zeros((1, E), f32)], axis=1)
        star[i * 7 + 6] = jnp.broadcast_to(tile, (8, 128))
    roots = []
    for i in range(Q):
        roots.append(jnp.concatenate([root[i, :, f, :] for f in range(4)], axis=1))
        row = jnp.concatenate([plus_in[i, :, f, :] for f in range(4)], axis=1) * rate4
        for j in range(Q):
            plus[i * Q + j] = jnp.broadcast_to(row[j : j + 1], (8, 128))
    for i in range(Q):
        for j in range(i, Q):
            row = jnp.sum(roots[i] * roots[j], axis=0, keepdims=True) * rate4
            row = jnp.broadcast_to(row, (8, 128))
            minus[i * Q + j] = row
            minus[j * Q + i] = row
    stiff_rows = [stiff[d] - jnp.transpose(stiff[d], (1, 0)) for d in range(3)]
    stiff_rows = jnp.concatenate(stiff_rows + [jnp.zeros((M, K3 - 3 * M), f32)], axis=1)
    s_stack[...] = stacked(jnp.concatenate([stiff_rows, jnp.zeros((8, K3), f32)], axis=0))
    p_rows[...] = jnp.zeros_like(p_rows)
    for f in range(4):
        p_rows[f * FM : f * FM + 21, 0:M] = proj[:, f, :]
    p_stack[...] = stacked(p_rows[...])
    pt_stack[...] = stacked(jnp.transpose(p_rows[...], (1, 0)))
    for u in range(STEPS):
        first = [kind12 == 2, kind12 == 1]
        starting = (True, first[0], first[0] | first[1], first[0])[u]
        mask[u] = jnp.ones((8, W), f32) if u == 0 else jnp.where(starting, 1.0, 0.0).astype(f32)
        for k in range(TERMS):
            coef[u * TERMS + k] = jnp.where(
                first[0],
                weights(k, 0),
                jnp.where(first[1], weights(k, u % 2), weights(k, u)),
            ).astype(f32)
    code = jnp.concatenate([codes[0, f : f + 1, :] for f in range(4)], axis=1)
    local = lax.broadcasted_iota(jnp.int32, (128, 128), 0) == code
    local = jnp.where(local, 1.0, 0.0).astype(f32).astype(bf16)
    pick[...] = jnp.concatenate([local, local], axis=0)
    remote = lax.broadcasted_iota(jnp.int32, (32, 128), 0) + 128 == code
    remote = jnp.where(remote, 1.0, 0.0).astype(f32).astype(bf16)
    owed[...] = jnp.concatenate([remote, remote], axis=1)
    base[...] = jnp.zeros_like(base)
    base[:, 0 : Q * E] = jnp.transpose(dofs[...].reshape(Q * E, M), (1, 0))
    pending[...] = jnp.zeros_like(pending)

    def tall(row):
        return jnp.broadcast_to(row[None], (M // 8, 8, W)).reshape(M, W)

    def exchange(u, p, slot):
        return pltpu.make_async_remote_copy(
            src_ref=send_buf.at[u, p],
            dst_ref=recv_buf.at[u, slot],
            send_sem=send_sem.at[u, p],
            recv_sem=recv_sem.at[u, slot],
            device_id=links[p][1],
            device_id_type=MESH,
        )

    def send(u, p):
        exchange(u, p, links[p][2]).start()

    def collect(u, p):
        exchange(u, p, links[p][2]).wait_send()
        exchange(u, p, p).wait_recv()

    def fixed(p):
        return pltpu.make_async_remote_copy(
            src_ref=fixed_send,
            dst_ref=fixed_recv,
            send_sem=fixed_sem.at[0],
            recv_sem=fixed_sem.at[1],
            device_id=links[p][1],
            device_id_type=MESH,
        )

    def expand(u, x, table):
        def term(k, carry):
            x, total = carry
            x = operator(x, table, s_stack)
            return x, total + tall(coef[u * TERMS + k]) * x

        return lax.fori_loop(1, TERMS, term, (x, tall(coef[u * TERMS]) * x))[1]

    def project(total):
        padded = jnp.concatenate([total, jnp.zeros((8, W), f32)], axis=0)
        traces = to_face_lanes(dot3(p_stack[...], padded))
        rows = jnp.concatenate(traces + [jnp.zeros((8, 128), f32)], axis=0)
        return traces, jnp.concatenate(split(rows), axis=1)

    def rows_for(places, both):
        return lax.dot_general(
            places, both, (((1,), (1,)), ((), ())), preferred_element_type=f32
        )

    def lifted(flux):
        return dot3(pt_stack[...], to_quantity_lanes(flux))[:M]

    def placed(rows, places, count):
        hi, lo = split(jnp.transpose(rows, (1, 0))[:count])
        return jnp.dot(hi, places, preferred_element_type=f32) + jnp.dot(
            lo, places, preferred_element_type=f32
        )

    def received(rows, places, table):
        taken = placed(rows, places, 224)
        return lifted(contract([taken[q * FM : q * FM + FM] for q in range(Q)], table))

    def absorb():
        pending[...] += received(inbox[...], owed[:, 0:128], plus)

    def stay(u, traces, both):
        taken = jnp.dot(both, pick[...], preferred_element_type=f32)
        taken = [taken[q * FM : q * FM + FM] for q in range(Q)]
        flux = [a - b for a, b in zip(contract(taken, plus), contract(traces, minus))]
        pending[...] = (
            jnp.where(tall(mask[u]) > 0.5, 0.0, pending[...])
            + operator(portion[...], star, s_stack)
            + lifted(flux)
        )

    def pack_fixed():
        for p, there in far.items():

            @pl.when(there)
            def _():
                v = owed[:, 0:128].astype(f32)[p * 8 : p * 8 + 8]
                v = v + pltpu.roll(v, 64, 1)
                v = v + pltpu.roll(v, 32, 1)
                lane = lax.broadcasted_iota(jnp.int32, (8, 128), 1) // E
                chosen = [jnp.where(lane == g, v, 0.0) for g in range(4)]
                chosen = jnp.concatenate(chosen, axis=0).astype(bf16)
                rows = jnp.concatenate([star[:, 0, :], jnp.zeros((1, 128), f32)], axis=0)
                hi, lo = split(rows)
                rows = rows_for(chosen, hi) + rows_for(chosen, lo)
                rows = jnp.concatenate([rows, jnp.zeros((32, 64), f32)], axis=1)
                fixed_send[0:16] = rows[:16] + pltpu.roll(rows[16:], 64, 1)
                lane = lax.broadcasted_iota(jnp.int32, (1, 128), 1)
                fast = jnp.where(kind4 == 2, 1.0, 0.0).astype(f32)
                rows = jnp.concatenate(
                    [
                        plus[:, 0, :] * fast,
                        (lane % E).astype(f32),
                        (lane // E).astype(f32),
                        jnp.zeros((45, 128), f32),
                    ],
                    axis=0,
                )
                rows = rows_for(owed[...], jnp.concatenate(split(rows), axis=1))
                fixed_send[16:24] = rows[p * 8 : p * 8 + 8]

    def unpack_fixed():
        for p, there in far.items():

            @pl.when(there)
            def _():
                fixed(p).wait_send()
                fixed(p).wait_recv()
                row = lax.broadcasted_iota(jnp.int32, (32, 128), 0)
                lane = lax.broadcasted_iota(jnp.int32, (32, 128), 1)
                wide = (lane // E == row // 8) & (lane % E == p * 8 + row % 8)
                wide = jnp.where(wide, 1.0, 0.0).astype(f32).astype(bf16)
                rows = fixed_recv[0:16]
                rows = jnp.concatenate([rows, pltpu.roll(rows, 64, 1)], axis=0)
                rows = placed(rows, wide, 64)
                for r in range(63):
                    far_star[r] = jnp.broadcast_to(rows[r : r + 1], (8, 128))
                rows = fixed_recv[16:24]
                lane = lax.broadcasted_iota(jnp.int32, (8, 128), 1).astype(f32)
                element, face = rows[:, 81:82], rows[:, 82:83]
                owner = jnp.where(lane == element, 1.0, 0.0).astype(f32).astype(bf16)
                same = rows_for(owner, owner)
                order = lax.broadcasted_iota(jnp.int32, (8, 8), 1).astype(f32)
                leader = jnp.min(jnp.where(same > 0.5, order, 8.0), axis=1, keepdims=True)
                spot = jnp.where(lane == face * E + (p * 8) + leader, 1.0, 0.0).astype(f32)
                blank = [jnp.zeros((8, 128), f32)]
                spots = jnp.concatenate(blank * p + [spot] + blank * (3 - p), axis=0).astype(bf16)
                far_place[...] = jnp.concatenate([spots, spots], axis=1)
                rows = jnp.concatenate(blank * p + [rows] + blank * (3 - p), axis=0)
                rows = placed(rows, spots, 88)
                for r in range(81):
                    far_plus[r] = jnp.broadcast_to(rows[r : r + 1], (8, 128))

    def respond(u):
        mine = send_buf[u].reshape(32, 256)
        x = received(mine, far_place[:, 0:128], far_plus)
        both = project(expand(0, x, far_star))[1]
        answer[:, 0:224] = rows_for(far_place[...], both)

    def pair(h, _):
        u, v = 2 * h, 2 * h + 1
        total = expand(u, base[...], star)
        portion[...] = total
        traces, both = project(total)
        outgoing = rows_for(owed[...], both)
        for p in range(4):
            send_buf[u, p, :, 0:224] = outgoing[p * 8 : p * 8 + 8]

        @pl.when(h == 0)
        def _():
            pack_fixed()
            pl.semaphore_wait(barrier, sum(there.astype(jnp.int32) for there, _, _ in links))

        for p in (3, 2, 0, 1):

            @pl.when(links[p][0])
            def _():
                send(u, p)

        for p, there in far.items():

            @pl.when(there & (h == 0))
            def _():
                fixed(p).start()

        stay(u, traces, both)
        inbox[...] = jnp.zeros_like(inbox)
        for p in range(4):

            @pl.when(near[p])
            def _():
                collect(u, p)
                inbox[p * 8 : p * 8 + 8] = recv_buf[u, p]

        absorb()

        @pl.when(is_far)
        def _():
            x = jnp.where(tall(mask[v]) > 0.5, base[...] + pending[...], base[...])
            early = rows_for(owed[...], project(expand(v, x, star))[1])
            for p, there in far.items():

                @pl.when(there)
                def _():
                    send_buf[v, p, :, 0:224] = early[p * 8 : p * 8 + 8]
                    send(v, p)

            @pl.when(h > 0)
            def _():
                respond(u)

            inbox[...] = jnp.zeros_like(inbox)
            for p, there in far.items():

                @pl.when(there)
                def _():
                    collect(u, p)
                    inbox[p * 8 : p * 8 + 8] = recv_buf[u, p]

            absorb()

        x = jnp.where(tall(mask[v]) > 0.5, base[...] + pending[...], base[...])
        base[...] = x
        total = expand(v, x, star)
        portion[...] = total
        traces, both = project(total)
        outgoing = rows_for(owed[...], both)
        for p in range(4):

            @pl.when(near[p])
            def _():
                send_buf[v, p, :, 0:224] = outgoing[p * 8 : p * 8 + 8]
                send(v, p)

        stay(v, traces, both)
        inbox[...] = jnp.zeros_like(inbox)

        @pl.when(is_far)
        def _():
            @pl.when(h == 0)
            def _():
                unpack_fixed()
                respond(u)

            for p, there in far.items():

                @pl.when(there)
                def _():
                    collect(v, p)
                    rows = slice(p * 8, p * 8 + 8)
                    inbox[rows, 0:224] = recv_buf[v, p, :, 0:224] + answer[rows, 0:224]

        for p in range(4):

            @pl.when(near[p])
            def _():
                collect(v, p)
                inbox[p * 8 : p * 8 + 8] = recv_buf[v, p]

        absorb()
        last = h == STEPS // 2 - 1
        following = jnp.minimum(v + 1, STEPS - 1)
        ending = (tall(mask[following]) > 0.5) | last
        base[...] = jnp.where(ending, base[...] + pending[...], base[...])
        return 0

    lax.fori_loop(0, STEPS // 2, pair, 0)
    out[...] = jnp.transpose(base[:, 0 : Q * E], (1, 0)).reshape(Q, E, M)


def on_device(dofs, jac, stiff, proj, root, plus_in, cluster, codes, send_faces):
    axes = (lax.axis_size("group"), lax.axis_size("dev"))
    scratch = [
        pltpu.VMEM((Q, E, M), f32),
        pltpu.VMEM((Q, Q, 3, E), f32),
        pltpu.VMEM((3, M, M), f32),
        pltpu.VMEM((21, 4, M), f32),
        pltpu.VMEM((Q, Q, 4, E), f32),
        pltpu.VMEM((Q, Q, 4, E), f32),
        pltpu.VMEM((1, E), jnp.int32),
        pltpu.VMEM((2, 4, E), jnp.int32),
        pltpu.SemaphoreType.DMA((8,)),
        pltpu.VMEM((63, 8, 128), f32),
        pltpu.VMEM((81, 8, 128), f32),
        pltpu.VMEM((81, 8, 128), f32),
        pltpu.VMEM((128, K3), bf16),
        pltpu.VMEM((8 * FM, 64), bf16),
        pltpu.VMEM((128, 4 * FM), bf16),
        pltpu.VMEM((4 * FM, 64), f32),
        pltpu.VMEM((STEPS * TERMS, 8, W), f32),
        pltpu.VMEM((STEPS, 8, W), f32),
        pltpu.VMEM((256, 128), bf16),
        pltpu.VMEM((32, 256), bf16),
        pltpu.VMEM((M, W), f32),
        pltpu.VMEM((M, W), f32),
        pltpu.VMEM((M, W), f32),
        pltpu.VMEM((32, 256), f32),
        pltpu.VMEM((STEPS, 4, 8, 256), f32),
        pltpu.VMEM((STEPS, 4, 8, 256), f32),
        pltpu.VMEM((24, 128), f32),
        pltpu.VMEM((24, 128), f32),
        pltpu.VMEM((63, 8, 128), f32),
        pltpu.VMEM((81, 8, 128), f32),
        pltpu.VMEM((32, 256), bf16),
        pltpu.VMEM((32, 256), f32),
        pltpu.SemaphoreType.DMA((STEPS, 4)),
        pltpu.SemaphoreType.DMA((STEPS, 4)),
        pltpu.SemaphoreType.DMA((2,)),
    ]
    final = pl.pallas_call(
        functools.partial(kernel, axes),
        out_shape=jax.ShapeDtypeStruct((Q, E, M), f32),
        in_specs=[pl.BlockSpec(memory_space=pl.ANY)] * 8,
        out_specs=pl.BlockSpec(memory_space=pltpu.VMEM),
        scratch_shapes=scratch,
        compiler_params=pltpu.CompilerParams(collective_id=0, has_side_effects=True),
        name="lts_update",
    )(
        jnp.transpose(dofs, (1, 2, 0)),
        jnp.transpose(jac, (1, 2, 0, 3)),
        stiff,
        jnp.transpose(proj, (1, 0, 2)),
        jnp.transpose(root, (1, 2, 0, 3)),
        jnp.transpose(plus_in, (1, 2, 0, 3)),
        cluster.reshape(1, E),
        codes,
    )
    return jnp.transpose(final, (2, 0, 1))


def solution(mesh):
    placed = (
        P(None, None, ("group", "dev")),
        P(None, None, None, ("group", "dev")),
        P(),
        P(),
        P(None, None, None, ("group", "dev")),
        P(None, None, None, ("group", "dev")),
        P(("group", "dev")),
        P(None, None, ("group", "dev")),
        P(None, ("group", "dev")),
    )
    return jax.shard_map(
        on_device,
        mesh=mesh,
        in_specs=placed,
        out_specs=P(None, None, ("group", "dev")),
        check_vma=False,
    )
```

```python
import functools
import math

import jax
import jax.numpy as jnp
from jax import lax
from jax.experimental import pallas as pl
from jax.experimental.pallas import tpu as pltpu
from jax.sharding import PartitionSpec as P

TERMS = 6
STEPS = 4
MESH = pl.DeviceIdType.MESH
f32, bf16 = jnp.float32, jnp.bfloat16

M, Q, E, FM = 56, 9, 32, 24
W = 384
K3 = 176
TR = 216


def weights(power, offset):
    start, end = offset * 0.25, offset * 0.25 + 0.25
    return (end ** (power + 1) - start ** (power + 1)) / math.factorial(power + 1)


def split(x):
    hi = x.astype(bf16)
    return hi, (x - hi.astype(f32)).astype(bf16)


def stacked(x):
    return jnp.concatenate(split(x), axis=0)


def dot3(stack, x):
    rows = stack.shape[0] // 2
    hi, lo = split(x)
    both = jnp.dot(stack, hi, preferred_element_type=f32)
    return both[:rows] + both[rows:] + jnp.dot(stack[:rows], lo, preferred_element_type=f32)


def lane_group(rows):
    return lax.broadcasted_iota(jnp.int32, (rows, 128), 1) // E


def spread(v):
    group = lane_group(v.shape[0])
    odd, high = (group % 2) == 1, group >= 2
    even = jnp.where(odd, pltpu.roll(v, 32, 1), v)
    other = jnp.where(odd, v, pltpu.roll(v, 96, 1))
    even_r, other_r = pltpu.roll(even, 64, 1), pltpu.roll(other, 64, 1)
    return (
        jnp.where(high, even_r, even),
        jnp.where(high, other_r, other),
        jnp.where(high, even, even_r),
        jnp.where(high, other, other_r),
    )


def quad(stack, y):
    rows = stack.shape[0] // 2
    both = jnp.dot(stack, jnp.concatenate(split(y), axis=1), preferred_element_type=f32)
    return (both[:rows, :128] + both[rows:, :128]) + (both[:rows, 128:] + both[rows:, 128:])


def operator(x, star, s_stack):
    tiles = M // 8
    wide = []
    for tile in range(tiles):
        rows = x[tile * 8 : tile * 8 + 8]
        wide.append(
            (*spread(rows[:, :128]), *spread(rows[:, 128:256]), spread(rows[:, 256:])[0])
        )

    def weighted(tile, at):
        total = wide[tile][0] * star[at]
        for i in range(1, Q):
            total = total + wide[tile][i] * star[i * 7 + at]
        return total

    blank = [jnp.zeros((8, 128), f32)]
    last = [weighted(tile, 6) for tile in range(tiles)]
    rolled = [pltpu.roll(y, 96, 1) for y in last] + [pltpu.roll(y, 64, 1) for y in last]
    stack = s_stack[...]
    out = [quad(stack, jnp.concatenate(last + rolled + blank, axis=0))]
    for t in range(2):
        y = [weighted(tile, d * 2 + t) for d in range(3) for tile in range(tiles)]
        out.append(quad(stack, jnp.concatenate(y + blank, axis=0)))
    return jnp.concatenate([out[1][:M], out[2][:M], out[0][:M]], axis=1)


def to_face_lanes(t):
    group = lane_group(FM)
    out = []
    for q in range(Q):
        tile, g = q // 4, q % 4
        cut = slice(tile * 128, tile * 128 + 128)
        total = None
        for f in range(4):
            piece = t[f * FM : f * FM + FM, cut]
            piece = pltpu.roll(piece, (32 * (f - g)) % 128, 1) if f != g else piece
            total = piece if total is None else jnp.where(group == f, piece, total)
        out.append(total)
    return out


def to_quantity_lanes(flux):
    group = lane_group(FM)
    rows = []
    for f in range(4):
        lanes = []
        for t in range(3):
            total = jnp.zeros((FM, 128), f32)
            for j in range(4 * t, min(4 * t + 4, Q)):
                g = j % 4
                piece = pltpu.roll(flux[j], (32 * (g - f)) % 128, 1) if f != g else flux[j]
                total = jnp.where(group == g, piece, total)
            lanes.append(total)
        rows.append(jnp.concatenate(lanes, axis=1))
    return jnp.concatenate(rows, axis=0)


def contract(rows, table):
    out = []
    for j in range(Q):
        total = None
        for i in range(Q):
            left = rows[i].reshape(FM // 8, 8, 128)
            term = left * table[i * Q + j][None]
            total = term if total is None else total + term
        out.append(total.reshape(FM, 128))
    return out


def kernel(
    axes,
    *refs,
):
    inputs, (out, *refs) = refs[:8], refs[8:]
    held, copy_sem, refs = refs[:8], refs[8], refs[9:]
    copies = [pltpu.make_async_copy(a, b, copy_sem.at[i]) for i, (a, b) in enumerate(zip(inputs, held))]
    body(axes, copies, *held, out, *refs)


def body(
    axes,
    copies,
    dofs,
    jac,
    stiff,
    proj,
    root,
    plus_in,
    cluster,
    codes,
    out,
    star,
    minus,
    plus,
    s_stack,
    p_stack,
    pt_stack,
    p_rows,
    coef,
    mask,
    pick,
    owed,
    base,
    portion,
    pending,
    inbox,
    send_buf,
    recv_buf,
    fixed_send,
    fixed_recv,
    far_star,
    far_plus,
    far_place,
    answer,
    send_sem,
    recv_sem,
    fixed_sem,
    relay_rows,
    relay_fixed,
    relay_sem,
    onward_sem,
):
    group, dev = lax.axis_index("group"), lax.axis_index("dev")
    n_group, n_dev = axes
    half = n_dev // 2
    links = (
        (group > 0, {"group": group - 1}, 1),
        (group < n_group - 1, {"group": group + 1}, 0),
        (dev > 0, {"dev": dev - 1}, 3),
        (dev < n_dev - 1, {"dev": dev + 1}, 2),
    )
    far = {2: dev == half, 3: dev == half - 1}
    is_far = (dev == half) | (dev == half - 1)
    near = [links[0][0], links[1][0], (dev > 0) & (dev != half)]
    near.append((dev < n_dev - 1) & (dev != half - 1))
    middle = n_group // 2
    giver = (dev == half - 1) & (group < middle)
    taker = (dev == half) & (group < middle)
    relay = (dev == half - 2) & (group >= middle)
    barrier = pltpu.get_barrier_semaphore()

    def greet(there, peer):
        @pl.when(there)
        def _():
            pl.semaphore_signal(barrier, inc=1, device_id=peer, device_id_type=MESH)

    for p, (there, peer, _) in enumerate(links):
        greet(there & jnp.logical_not(taker) if p == 2 else there, peer)
    above = {"group": group + middle, "dev": half - 2}
    greet(giver | taker, above)
    greet(relay, {"group": group - middle, "dev": half - 1})
    greet(relay, {"group": group - middle, "dev": half})
    callers = sum(there.astype(jnp.int32) for there, _, _ in links)
    callers = callers + taker.astype(jnp.int32) + 2 * relay.astype(jnp.int32)

    for copy in copies:
        copy.start()
    send_buf[...] = jnp.zeros_like(send_buf)
    fixed_send[...] = jnp.zeros_like(fixed_send)

    for copy in copies:
        copy.wait()

    kind = cluster[...]
    rate = jnp.where(kind == 2, 4.0, jnp.where(kind == 1, 2.0, 1.0)).astype(f32)
    rate4 = jnp.concatenate([rate] * 4, axis=1)
    kind4 = jnp.concatenate([kind] * 4, axis=1)
    kind12 = jnp.broadcast_to(jnp.concatenate([kind4] * 3, axis=1), (8, W))
    last = [[] for _ in range(Q)]
    for d in range(3):
        for i in range(Q):
            row = [
                0.5 * rate * (jac[i, j, d : d + 1, :] + jac[j, i, d : d + 1, :]) for j in range(Q)
            ]
            last[i].append(row[8])
            for t in range(2):
                tile = jnp.concatenate(row[4 * t : 4 * t + 4], axis=1)
                star[i * 7 + d * 2 + t] = jnp.broadcast_to(tile, (8, 128))
    for i in range(Q):
        tile = jnp.concatenate(last[i] + [jnp.zeros((1, E), f32)], axis=1)
        star[i * 7 + 6] = jnp.broadcast_to(tile, (8, 128))
    roots = []
    for i in range(Q):
        roots.append(jnp.concatenate([root[i, :, f, :] for f in range(4)], axis=1))
        row = jnp.concatenate([plus_in[i, :, f, :] for f in range(4)], axis=1) * rate4
        for j in range(Q):
            plus[i * Q + j] = jnp.broadcast_to(row[j : j + 1], (8, 128))
    for i in range(Q):
        for j in range(i, Q):
            row = jnp.sum(roots[i] * roots[j], axis=0, keepdims=True) * rate4
            row = jnp.broadcast_to(row, (8, 128))
            minus[i * Q + j] = row
            minus[j * Q + i] = row
    stiff_rows = [stiff[d] - jnp.transpose(stiff[d], (1, 0)) for d in range(3)]
    stiff_rows = jnp.concatenate(stiff_rows + [jnp.zeros((M, K3 - 3 * M), f32)], axis=1)
    s_stack[...] = stacked(jnp.concatenate([stiff_rows, jnp.zeros((8, K3), f32)], axis=0))
    p_rows[...] = jnp.zeros_like(p_rows)
    for f in range(4):
        p_rows[f * FM : f * FM + 21, 0:M] = proj[:, f, :]
    p_stack[...] = stacked(p_rows[...])
    pt_stack[...] = stacked(jnp.transpose(p_rows[...], (1, 0)))
    for u in range(STEPS):
        first = [kind12 == 2, kind12 == 1]
        starting = (True, first[0], first[0] | first[1], first[0])[u]
        mask[u] = jnp.ones((8, W), f32) if u == 0 else jnp.where(starting, 1.0, 0.0).astype(f32)
        for k in range(TERMS):
            coef[u * TERMS + k] = jnp.where(
                first[0],
                weights(k, 0),
                jnp.where(first[1], weights(k, u % 2), weights(k, u)),
            ).astype(f32)
    code = jnp.concatenate([codes[0, f : f + 1, :] for f in range(4)], axis=1)
    local = lax.broadcasted_iota(jnp.int32, (128, 128), 0) == code
    local = jnp.where(local, 1.0, 0.0).astype(f32).astype(bf16)
    pick[...] = jnp.concatenate([local, local], axis=0)
    remote = lax.broadcasted_iota(jnp.int32, (32, 128), 0) + 128 == code
    remote = jnp.where(remote, 1.0, 0.0).astype(f32).astype(bf16)
    owed[...] = jnp.concatenate([remote, remote], axis=1)
    base[...] = jnp.zeros_like(base)
    base[:, 0 : Q * E] = jnp.transpose(dofs[...].reshape(Q * E, M), (1, 0))
    pending[...] = jnp.zeros_like(pending)

    def tall(row):
        return jnp.broadcast_to(row[None], (M // 8, 8, W)).reshape(M, W)

    def exchange(u, p, slot):
        return pltpu.make_async_remote_copy(
            src_ref=send_buf.at[u, p],
            dst_ref=recv_buf.at[u, slot],
            send_sem=send_sem.at[u, p],
            recv_sem=recv_sem.at[u, slot],
            device_id=links[p][1],
            device_id_type=MESH,
        )

    def send(u, p):
        exchange(u, p, links[p][2]).start()

    def collect(u, p):
        exchange(u, p, links[p][2]).wait_send()
        exchange(u, p, p).wait_recv()

    def fixed(p):
        return pltpu.make_async_remote_copy(
            src_ref=fixed_send,
            dst_ref=fixed_recv,
            send_sem=fixed_sem.at[0],
            recv_sem=fixed_sem.at[1],
            device_id=links[p][1],
            device_id_type=MESH,
        )

    def hand_over(part):
        return pltpu.make_async_remote_copy(
            src_ref=(send_buf.at[0, 3], fixed_send, send_buf.at[1, 3])[part],
            dst_ref=(relay_rows.at[0], relay_fixed, relay_rows.at[1])[part],
            send_sem=(send_sem.at[0, 3], fixed_sem.at[0], send_sem.at[1, 3])[part],
            recv_sem=relay_sem.at[part],
            device_id=above,
            device_id_type=MESH,
        )

    def hand_on(part):
        return pltpu.make_async_remote_copy(
            src_ref=(relay_rows.at[0], relay_fixed, relay_rows.at[1])[part],
            dst_ref=(recv_buf.at[0, 2], fixed_recv, recv_buf.at[1, 2])[part],
            send_sem=onward_sem.at[part],
            recv_sem=(recv_sem.at[0, 2], fixed_sem.at[1], recv_sem.at[1, 2])[part],
            device_id={"group": group - middle, "dev": half},
            device_id_type=MESH,
        )

    def expand(u, x, table):
        def term(k, carry):
            x, total = carry
            x = operator(x, table, s_stack)
            return x, total + tall(coef[u * TERMS + k]) * x

        return lax.fori_loop(1, TERMS, term, (x, tall(coef[u * TERMS]) * x))[1]

    def project(total):
        padded = jnp.concatenate([total, jnp.zeros((8, W), f32)], axis=0)
        traces = to_face_lanes(dot3(p_stack[...], padded))
        rows = jnp.concatenate(traces + [jnp.zeros((8, 128), f32)], axis=0)
        return traces, jnp.concatenate(split(rows), axis=1)

    def rows_for(places, both):
        return lax.dot_general(
            places, both, (((1,), (1,)), ((), ())), preferred_element_type=f32
        )

    def lifted(flux):
        return dot3(pt_stack[...], to_quantity_lanes(flux))[:M]

    def placed(rows, places, count):
        hi, lo = split(jnp.transpose(rows, (1, 0))[:count])
        return jnp.dot(hi, places, preferred_element_type=f32) + jnp.dot(
            lo, places, preferred_element_type=f32
        )

    def received(rows, places, table):
        taken = placed(rows, places, 224)
        return lifted(contract([taken[q * FM : q * FM + FM] for q in range(Q)], table))

    def absorb():
        pending[...] += received(inbox[...], owed[:, 0:128], plus)

    def stay(u, traces, both):
        taken = jnp.dot(both, pick[...], preferred_element_type=f32)
        taken = [taken[q * FM : q * FM + FM] for q in range(Q)]
        flux = [a - b for a, b in zip(contract(taken, plus), contract(traces, minus))]
        pending[...] = (
            jnp.where(tall(mask[u]) > 0.5, 0.0, pending[...])
            + operator(portion[...], star, s_stack)
            + lifted(flux)
        )

    def pack_fixed():
        for p, there in far.items():

            @pl.when(there)
            def _():
                v = owed[:, 0:128].astype(f32)[p * 8 : p * 8 + 8]
                v = v + pltpu.roll(v, 64, 1)
                v = v + pltpu.roll(v, 32, 1)
                lane = lax.broadcasted_iota(jnp.int32, (8, 128), 1) // E
                chosen = [jnp.where(lane == g, v, 0.0) for g in range(4)]
                chosen = jnp.concatenate(chosen, axis=0).astype(bf16)
                rows = jnp.concatenate([star[:, 0, :], jnp.zeros((1, 128), f32)], axis=0)
                hi, lo = split(rows)
                rows = rows_for(chosen, hi) + rows_for(chosen, lo)
                rows = jnp.concatenate([rows, jnp.zeros((32, 64), f32)], axis=1)
                fixed_send[0:16] = rows[:16] + pltpu.roll(rows[16:], 64, 1)
                lane = lax.broadcasted_iota(jnp.int32, (1, 128), 1)
                fast = jnp.where(kind4 == 2, 1.0, 0.0).astype(f32)
                rows = jnp.concatenate(
                    [
                        plus[:, 0, :] * fast,
                        (lane % E).astype(f32),
                        (lane // E).astype(f32),
                        jnp.zeros((45, 128), f32),
                    ],
                    axis=0,
                )
                rows = rows_for(owed[...], jnp.concatenate(split(rows), axis=1))
                fixed_send[16:24] = rows[p * 8 : p * 8 + 8]

    def unpack_fixed():
        for p, there in far.items():

            @pl.when(there)
            def _():
                fixed(p).wait_send()
                fixed(p).wait_recv()
                row = lax.broadcasted_iota(jnp.int32, (32, 128), 0)
                lane = lax.broadcasted_iota(jnp.int32, (32, 128), 1)
                wide = (lane // E == row // 8) & (lane % E == p * 8 + row % 8)
                wide = jnp.where(wide, 1.0, 0.0).astype(f32).astype(bf16)
                rows = fixed_recv[0:16]
                rows = jnp.concatenate([rows, pltpu.roll(rows, 64, 1)], axis=0)
                rows = placed(rows, wide, 64)
                for r in range(63):
                    far_star[r] = jnp.broadcast_to(rows[r : r + 1], (8, 128))
                rows = fixed_recv[16:24]
                lane = lax.broadcasted_iota(jnp.int32, (8, 128), 1).astype(f32)
                element, face = rows[:, 81:82], rows[:, 82:83]
                owner = jnp.where(lane == element, 1.0, 0.0).astype(f32).astype(bf16)
                same = rows_for(owner, owner)
                order = lax.broadcasted_iota(jnp.int32, (8, 8), 1).astype(f32)
                leader = jnp.min(jnp.where(same > 0.5, order, 8.0), axis=1, keepdims=True)
                spot = jnp.where(lane == face * E + (p * 8) + leader, 1.0, 0.0).astype(f32)
                blank = [jnp.zeros((8, 128), f32)]
                spots = jnp.concatenate(blank * p + [spot] + blank * (3 - p), axis=0).astype(bf16)
                far_place[...] = jnp.concatenate([spots, spots], axis=1)
                rows = jnp.concatenate(blank * p + [rows] + blank * (3 - p), axis=0)
                rows = placed(rows, spots, 88)
                for r in range(81):
                    far_plus[r] = jnp.broadcast_to(rows[r : r + 1], (8, 128))

    def respond(u):
        mine = send_buf[u].reshape(32, 256)
        x = received(mine, far_place[:, 0:128], far_plus)
        both = project(expand(0, x, far_star))[1]
        answer[:, 0:224] = rows_for(far_place[...], both)

    def pair(h, _):
        u, v = 2 * h, 2 * h + 1
        total = expand(u, base[...], star)
        portion[...] = total
        traces, both = project(total)
        outgoing = rows_for(owed[...], both)
        for p in range(4):
            send_buf[u, p, :, 0:224] = outgoing[p * 8 : p * 8 + 8]

        @pl.when(h == 0)
        def _():
            pl.semaphore_wait(barrier, callers)

        by_relay = giver & (h == 0)

        @pl.when(by_relay)
        def _():
            hand_over(0).start()

        for p in (3, 2, 0, 1):
            there = links[p][0]

            @pl.when(there & jnp.logical_not(by_relay) if p == 3 else there)
            def _():
                send(u, p)

        @pl.when(h == 0)
        def _():
            pack_fixed()

        @pl.when(by_relay)
        def _():
            hand_over(1).start()

        for p, there in far.items():

            @pl.when(there & (h == 0) & jnp.logical_not(giver))
            def _():
                fixed(p).start()

        @pl.when(relay & (h == 0))
        def _():
            for part in range(2):
                hand_over(part).wait_recv()
                hand_on(part).start()

        stay(u, traces, both)

        @pl.when(relay & (h == 0))
        def _():
            hand_over(2).wait_recv()
            hand_on(2).start()

        inbox[...] = jnp.zeros_like(inbox)
        for p in range(4):

            @pl.when(near[p])
            def _():
                collect(u, p)
                inbox[p * 8 : p * 8 + 8] = recv_buf[u, p]

        absorb()

        @pl.when(is_far)
        def _():
            x = jnp.where(tall(mask[v]) > 0.5, base[...] + pending[...], base[...])
            early = rows_for(owed[...], project(expand(v, x, star))[1])
            for p, there in far.items():

                @pl.when(there)
                def _():
                    send_buf[v, p, :, 0:224] = early[p * 8 : p * 8 + 8]

                @pl.when(there & jnp.logical_not(by_relay) if p == 3 else there)
                def _():
                    send(v, p)

            @pl.when(by_relay)
            def _():
                hand_over(2).start()

            @pl.when(h > 0)
            def _():
                respond(u)

            inbox[...] = jnp.zeros_like(inbox)
            for p, there in far.items():

                @pl.when(there)
                def _():
                    collect(u, p)
                    inbox[p * 8 : p * 8 + 8] = recv_buf[u, p]

            absorb()

        x = jnp.where(tall(mask[v]) > 0.5, base[...] + pending[...], base[...])
        base[...] = x
        total = expand(v, x, star)
        portion[...] = total
        traces, both = project(total)
        outgoing = rows_for(owed[...], both)
        for p in range(4):

            @pl.when(near[p])
            def _():
                send_buf[v, p, :, 0:224] = outgoing[p * 8 : p * 8 + 8]
                send(v, p)

        stay(v, traces, both)
        inbox[...] = jnp.zeros_like(inbox)

        @pl.when(is_far)
        def _():
            @pl.when(h == 0)
            def _():
                unpack_fixed()
                respond(u)

            for p, there in far.items():

                @pl.when(there)
                def _():
                    collect(v, p)
                    rows = slice(p * 8, p * 8 + 8)
                    inbox[rows, 0:224] = recv_buf[v, p, :, 0:224] + answer[rows, 0:224]

        for p in range(4):

            @pl.when(near[p])
            def _():
                collect(v, p)
                inbox[p * 8 : p * 8 + 8] = recv_buf[v, p]

        absorb()
        last = h == STEPS // 2 - 1
        following = jnp.minimum(v + 1, STEPS - 1)
        ending = (tall(mask[following]) > 0.5) | last
        base[...] = jnp.where(ending, base[...] + pending[...], base[...])
        return 0

    lax.fori_loop(0, STEPS // 2, pair, 0)

    @pl.when(relay)
    def _():
        for part in range(3):
            hand_on(part).wait_send()

    out[...] = jnp.transpose(base[:, 0 : Q * E], (1, 0)).reshape(Q, E, M)


def on_device(dofs, jac, stiff, proj, root, plus_in, cluster, codes, send_faces):
    axes = (lax.axis_size("group"), lax.axis_size("dev"))
    scratch = [
        pltpu.VMEM((Q, E, M), f32),
        pltpu.VMEM((Q, Q, 3, E), f32),
        pltpu.VMEM((3, M, M), f32),
        pltpu.VMEM((21, 4, M), f32),
        pltpu.VMEM((Q, Q, 4, E), f32),
        pltpu.VMEM((Q, Q, 4, E), f32),
        pltpu.VMEM((1, E), jnp.int32),
        pltpu.VMEM((2, 4, E), jnp.int32),
        pltpu.SemaphoreType.DMA((8,)),
        pltpu.VMEM((63, 8, 128), f32),
        pltpu.VMEM((81, 8, 128), f32),
        pltpu.VMEM((81, 8, 128), f32),
        pltpu.VMEM((128, K3), bf16),
        pltpu.VMEM((8 * FM, 64), bf16),
        pltpu.VMEM((128, 4 * FM), bf16),
        pltpu.VMEM((4 * FM, 64), f32),
        pltpu.VMEM((STEPS * TERMS, 8, W), f32),
        pltpu.VMEM((STEPS, 8, W), f32),
        pltpu.VMEM((256, 128), bf16),
        pltpu.VMEM((32, 256), bf16),
        pltpu.VMEM((M, W), f32),
        pltpu.VMEM((M, W), f32),
        pltpu.VMEM((M, W), f32),
        pltpu.VMEM((32, 256), f32),
        pltpu.VMEM((STEPS, 4, 8, 256), f32),
        pltpu.VMEM((STEPS, 4, 8, 256), f32),
        pltpu.VMEM((24, 128), f32),
        pltpu.VMEM((24, 128), f32),
        pltpu.VMEM((63, 8, 128), f32),
        pltpu.VMEM((81, 8, 128), f32),
        pltpu.VMEM((32, 256), bf16),
        pltpu.VMEM((32, 256), f32),
        pltpu.SemaphoreType.DMA((STEPS, 4)),
        pltpu.SemaphoreType.DMA((STEPS, 4)),
        pltpu.SemaphoreType.DMA((2,)),
        pltpu.VMEM((2, 8, 256), f32),
        pltpu.VMEM((24, 128), f32),
        pltpu.SemaphoreType.DMA((3,)),
        pltpu.SemaphoreType.DMA((3,)),
    ]
    final = pl.pallas_call(
        functools.partial(kernel, axes),
        out_shape=jax.ShapeDtypeStruct((Q, E, M), f32),
        in_specs=[pl.BlockSpec(memory_space=pl.ANY)] * 8,
        out_specs=pl.BlockSpec(memory_space=pltpu.VMEM),
        scratch_shapes=scratch,
        compiler_params=pltpu.CompilerParams(collective_id=0, has_side_effects=True),
        name="lts_update",
    )(
        jnp.transpose(dofs, (1, 2, 0)),
        jnp.transpose(jac, (1, 2, 0, 3)),
        stiff,
        jnp.transpose(proj, (1, 0, 2)),
        jnp.transpose(root, (1, 2, 0, 3)),
        jnp.transpose(plus_in, (1, 2, 0, 3)),
        cluster.reshape(1, E),
        codes,
    )
    return jnp.transpose(final, (2, 0, 1))


def solution(mesh):
    placed = (
        P(None, None, ("group", "dev")),
        P(None, None, None, ("group", "dev")),
        P(),
        P(),
        P(None, None, None, ("group", "dev")),
        P(None, None, None, ("group", "dev")),
        P(("group", "dev")),
        P(None, None, ("group", "dev")),
        P(None, ("group", "dev")),
    )
    return jax.shard_map(
        on_device,
        mesh=mesh,
        in_specs=placed,
        out_specs=P(None, None, ("group", "dev")),
        check_vma=False,
    )
```

```python
import functools
import math

import jax
import jax.numpy as jnp
from jax import lax
from jax.experimental import pallas as pl
from jax.experimental.pallas import tpu as pltpu
from jax.sharding import PartitionSpec as P

TERMS = 6
STEPS = 4
MESH = pl.DeviceIdType.MESH
f32, bf16 = jnp.float32, jnp.bfloat16

M, Q, E, FM = 56, 9, 32, 24
W = 384
K3 = 176
TR = 216


def weights(power, offset):
    start, end = offset * 0.25, offset * 0.25 + 0.25
    return (end ** (power + 1) - start ** (power + 1)) / math.factorial(power + 1)


def split(x):
    hi = x.astype(bf16)
    return hi, (x - hi.astype(f32)).astype(bf16)


def stacked(x):
    return jnp.concatenate(split(x), axis=0)


def dot3(stack, x):
    rows = stack.shape[0] // 2
    hi, lo = split(x)
    both = jnp.dot(stack, hi, preferred_element_type=f32)
    return both[:rows] + both[rows:] + jnp.dot(stack[:rows], lo, preferred_element_type=f32)


def lane_group(rows):
    return lax.broadcasted_iota(jnp.int32, (rows, 128), 1) // E


def spread(v):
    group = lane_group(v.shape[0])
    odd, high = (group % 2) == 1, group >= 2
    even = jnp.where(odd, pltpu.roll(v, 32, 1), v)
    other = jnp.where(odd, v, pltpu.roll(v, 96, 1))
    even_r, other_r = pltpu.roll(even, 64, 1), pltpu.roll(other, 64, 1)
    return (
        jnp.where(high, even_r, even),
        jnp.where(high, other_r, other),
        jnp.where(high, even, even_r),
        jnp.where(high, other, other_r),
    )


def quad(stack, y):
    rows = stack.shape[0] // 2
    both = jnp.dot(stack, jnp.concatenate(split(y), axis=1), preferred_element_type=f32)
    return (both[:rows, :128] + both[rows:, :128]) + (both[:rows, 128:] + both[rows:, 128:])


def operator(x, star, s_stack):
    tiles = M // 8
    wide = []
    for tile in range(tiles):
        rows = x[tile * 8 : tile * 8 + 8]
        wide.append(
            (*spread(rows[:, :128]), *spread(rows[:, 128:256]), spread(rows[:, 256:])[0])
        )

    def weighted(tile, at):
        total = wide[tile][0] * star[at]
        for i in range(1, Q):
            total = total + wide[tile][i] * star[i * 7 + at]
        return total

    blank = [jnp.zeros((8, 128), f32)]
    last = [weighted(tile, 6) for tile in range(tiles)]
    rolled = [pltpu.roll(y, 96, 1) for y in last] + [pltpu.roll(y, 64, 1) for y in last]
    stack = s_stack[...]
    out = [quad(stack, jnp.concatenate(last + rolled + blank, axis=0))]
    for t in range(2):
        y = [weighted(tile, d * 2 + t) for d in range(3) for tile in range(tiles)]
        out.append(quad(stack, jnp.concatenate(y + blank, axis=0)))
    return jnp.concatenate([out[1][:M], out[2][:M], out[0][:M]], axis=1)


def to_face_lanes(t):
    group = lane_group(FM)
    out = []
    for q in range(Q):
        tile, g = q // 4, q % 4
        cut = slice(tile * 128, tile * 128 + 128)
        total = None
        for f in range(4):
            piece = t[f * FM : f * FM + FM, cut]
            piece = pltpu.roll(piece, (32 * (f - g)) % 128, 1) if f != g else piece
            total = piece if total is None else jnp.where(group == f, piece, total)
        out.append(total)
    return out


def to_quantity_lanes(flux):
    group = lane_group(FM)
    rows = []
    for f in range(4):
        lanes = []
        for t in range(3):
            total = jnp.zeros((FM, 128), f32)
            for j in range(4 * t, min(4 * t + 4, Q)):
                g = j % 4
                piece = pltpu.roll(flux[j], (32 * (g - f)) % 128, 1) if f != g else flux[j]
                total = jnp.where(group == g, piece, total)
            lanes.append(total)
        rows.append(jnp.concatenate(lanes, axis=1))
    return jnp.concatenate(rows, axis=0)


def contract(rows, table):
    out = []
    for j in range(Q):
        total = None
        for i in range(Q):
            left = rows[i].reshape(FM // 8, 8, 128)
            term = left * table[i * Q + j][None]
            total = term if total is None else total + term
        out.append(total.reshape(FM, 128))
    return out


def kernel(
    axes,
    *refs,
):
    inputs, (out, *refs) = refs[:8], refs[8:]
    held, copy_sem, refs = refs[:8], refs[8], refs[9:]
    copies = [pltpu.make_async_copy(a, b, copy_sem.at[i]) for i, (a, b) in enumerate(zip(inputs, held))]
    body(axes, copies, *held, out, *refs)


def body(
    axes,
    copies,
    dofs,
    jac,
    stiff,
    proj,
    root,
    plus_in,
    cluster,
    codes,
    out,
    star,
    minus,
    plus,
    s_stack,
    p_stack,
    pt_stack,
    p_rows,
    coef,
    mask,
    pick,
    owed,
    base,
    portion,
    pending,
    inbox,
    send_buf,
    recv_buf,
    fixed_send,
    fixed_recv,
    far_star,
    far_plus,
    far_place,
    answer,
    send_sem,
    recv_sem,
    fixed_sem,
    relay_rows,
    relay_fixed,
    relay_sem,
    onward_sem,
):
    group, dev = lax.axis_index("group"), lax.axis_index("dev")
    n_group, n_dev = axes
    half = n_dev // 2
    links = (
        (group > 0, {"group": group - 1}, 1),
        (group < n_group - 1, {"group": group + 1}, 0),
        (dev > 0, {"dev": dev - 1}, 3),
        (dev < n_dev - 1, {"dev": dev + 1}, 2),
    )
    far = {2: dev == half, 3: dev == half - 1}
    is_far = (dev == half) | (dev == half - 1)
    near = [links[0][0], links[1][0], (dev > 0) & (dev != half)]
    near.append((dev < n_dev - 1) & (dev != half - 1))
    middle = n_group // 2
    giver = dev == half - 1
    taker = dev == half
    relay = ((dev == half - 2) & (group >= middle)) | ((dev == half + 2) & (group < middle))
    opposite = lax.rem(group + middle, n_group)
    barrier = pltpu.get_barrier_semaphore()

    def greet(there, peer):
        @pl.when(there)
        def _():
            pl.semaphore_signal(barrier, inc=1, device_id=peer, device_id_type=MESH)

    for p, (there, peer, _) in enumerate(links):
        greet(there & jnp.logical_not(taker) if p == 2 else there, peer)
    above = {"group": opposite, "dev": half - 2 + 4 * lax.div(group, middle)}
    greet(giver | taker, above)
    greet(relay, {"group": opposite, "dev": half - 1})
    greet(relay, {"group": opposite, "dev": half})
    callers = sum(there.astype(jnp.int32) for there, _, _ in links)
    callers = callers + taker.astype(jnp.int32) + 2 * relay.astype(jnp.int32)

    for copy in copies:
        copy.start()
    send_buf[...] = jnp.zeros_like(send_buf)
    fixed_send[...] = jnp.zeros_like(fixed_send)

    for copy in copies:
        copy.wait()

    kind = cluster[...]
    rate = jnp.where(kind == 2, 4.0, jnp.where(kind == 1, 2.0, 1.0)).astype(f32)
    rate4 = jnp.concatenate([rate] * 4, axis=1)
    kind4 = jnp.concatenate([kind] * 4, axis=1)
    kind12 = jnp.broadcast_to(jnp.concatenate([kind4] * 3, axis=1), (8, W))
    last = [[] for _ in range(Q)]
    for d in range(3):
        for i in range(Q):
            row = [
                0.5 * rate * (jac[i, j, d : d + 1, :] + jac[j, i, d : d + 1, :]) for j in range(Q)
            ]
            last[i].append(row[8])
            for t in range(2):
                tile = jnp.concatenate(row[4 * t : 4 * t + 4], axis=1)
                star[i * 7 + d * 2 + t] = jnp.broadcast_to(tile, (8, 128))
    for i in range(Q):
        tile = jnp.concatenate(last[i] + [jnp.zeros((1, E), f32)], axis=1)
        star[i * 7 + 6] = jnp.broadcast_to(tile, (8, 128))
    def late_tables():
        roots = []
        for i in range(Q):
            roots.append(jnp.concatenate([root[i, :, f, :] for f in range(4)], axis=1))
            row = jnp.concatenate([plus_in[i, :, f, :] for f in range(4)], axis=1) * rate4
            for j in range(Q):
                plus[i * Q + j] = jnp.broadcast_to(row[j : j + 1], (8, 128))
        for i in range(Q):
            for j in range(i, Q):
                row = jnp.sum(roots[i] * roots[j], axis=0, keepdims=True) * rate4
                row = jnp.broadcast_to(row, (8, 128))
                minus[i * Q + j] = row
                minus[j * Q + i] = row
        local = lax.broadcasted_iota(jnp.int32, (128, 128), 0) == code
        local = jnp.where(local, 1.0, 0.0).astype(f32).astype(bf16)
        pick[...] = jnp.concatenate([local, local], axis=0)
        pt_stack[...] = stacked(jnp.transpose(p_rows[...], (1, 0)))
        pending[...] = jnp.zeros_like(pending)
        for u in range(STEPS):
            starting = (True, fast, fast | middling, fast)[u]
            mask[u] = jnp.where(starting, 1.0, 0.0).astype(f32) if u else jnp.ones((8, W), f32)

    stiff_rows = [stiff[d] - jnp.transpose(stiff[d], (1, 0)) for d in range(3)]
    stiff_rows = jnp.concatenate(stiff_rows + [jnp.zeros((M, K3 - 3 * M), f32)], axis=1)
    s_stack[...] = stacked(jnp.concatenate([stiff_rows, jnp.zeros((8, K3), f32)], axis=0))
    p_rows[...] = jnp.zeros_like(p_rows)
    for f in range(4):
        p_rows[f * FM : f * FM + 21, 0:M] = proj[:, f, :]
    p_stack[...] = stacked(p_rows[...])
    fast, middling = kind12 == 2, kind12 == 1
    for u in range(STEPS):
        for k in range(TERMS):
            coef[u * TERMS + k] = jnp.where(
                fast,
                weights(k, 0),
                jnp.where(middling, weights(k, u % 2), weights(k, u)),
            ).astype(f32)
    code = jnp.concatenate([codes[0, f : f + 1, :] for f in range(4)], axis=1)
    remote = lax.broadcasted_iota(jnp.int32, (32, 128), 0) + 128 == code
    remote = jnp.where(remote, 1.0, 0.0).astype(f32).astype(bf16)
    owed[...] = jnp.concatenate([remote, remote], axis=1)
    base[...] = jnp.zeros_like(base)
    base[:, 0 : Q * E] = jnp.transpose(dofs[...].reshape(Q * E, M), (1, 0))

    def tall(row):
        return jnp.broadcast_to(row[None], (M // 8, 8, W)).reshape(M, W)

    def exchange(u, p, slot):
        return pltpu.make_async_remote_copy(
            src_ref=send_buf.at[u, p],
            dst_ref=recv_buf.at[u, slot],
            send_sem=send_sem.at[u, p],
            recv_sem=recv_sem.at[u, slot],
            device_id=links[p][1],
            device_id_type=MESH,
        )

    def send(u, p):
        exchange(u, p, links[p][2]).start()

    def collect(u, p):
        exchange(u, p, links[p][2]).wait_send()
        exchange(u, p, p).wait_recv()

    def fixed(p):
        return pltpu.make_async_remote_copy(
            src_ref=fixed_send,
            dst_ref=fixed_recv,
            send_sem=fixed_sem.at[0],
            recv_sem=fixed_sem.at[1],
            device_id=links[p][1],
            device_id_type=MESH,
        )

    def hand_over(part):
        return pltpu.make_async_remote_copy(
            src_ref=(send_buf.at[0, 3], fixed_send, send_buf.at[1, 3])[part],
            dst_ref=(relay_rows.at[0], relay_fixed, relay_rows.at[1])[part],
            send_sem=(send_sem.at[0, 3], fixed_sem.at[0], send_sem.at[1, 3])[part],
            recv_sem=relay_sem.at[part],
            device_id=above,
            device_id_type=MESH,
        )

    def hand_on(part):
        return pltpu.make_async_remote_copy(
            src_ref=(relay_rows.at[0], relay_fixed, relay_rows.at[1])[part],
            dst_ref=(recv_buf.at[0, 2], fixed_recv, recv_buf.at[1, 2])[part],
            send_sem=onward_sem.at[part],
            recv_sem=(recv_sem.at[0, 2], fixed_sem.at[1], recv_sem.at[1, 2])[part],
            device_id={"group": opposite, "dev": half},
            device_id_type=MESH,
        )

    def expand(u, x, table):
        def term(k, carry):
            x, total = carry
            x = operator(x, table, s_stack)
            return x, total + tall(coef[u * TERMS + k]) * x

        return lax.fori_loop(1, TERMS, term, (x, tall(coef[u * TERMS]) * x), unroll=True)[1]

    def project(total):
        padded = jnp.concatenate([total, jnp.zeros((8, W), f32)], axis=0)
        traces = to_face_lanes(dot3(p_stack[...], padded))
        rows = jnp.concatenate(traces + [jnp.zeros((8, 128), f32)], axis=0)
        return traces, jnp.concatenate(split(rows), axis=1)

    def rows_for(places, both):
        return lax.dot_general(
            places, both, (((1,), (1,)), ((), ())), preferred_element_type=f32
        )

    def lifted(flux):
        return dot3(pt_stack[...], to_quantity_lanes(flux))[:M]

    def placed(rows, places, count):
        hi, lo = split(jnp.transpose(rows, (1, 0))[:count])
        return jnp.dot(hi, places, preferred_element_type=f32) + jnp.dot(
            lo, places, preferred_element_type=f32
        )

    def received(rows, places, table):
        taken = placed(rows, places, 224)
        return lifted(contract([taken[q * FM : q * FM + FM] for q in range(Q)], table))

    def absorb():
        pending[...] += received(inbox[...], owed[:, 0:128], plus)

    def stay(u, traces, both):
        taken = jnp.dot(both, pick[...], preferred_element_type=f32)
        taken = [taken[q * FM : q * FM + FM] for q in range(Q)]
        flux = [a - b for a, b in zip(contract(taken, plus), contract(traces, minus))]
        pending[...] = (
            jnp.where(tall(mask[u]) > 0.5, 0.0, pending[...])
            + operator(portion[...], star, s_stack)
            + lifted(flux)
        )

    def pack_fixed():
        for p, there in far.items():

            @pl.when(there)
            def _():
                v = owed[:, 0:128].astype(f32)[p * 8 : p * 8 + 8]
                v = v + pltpu.roll(v, 64, 1)
                v = v + pltpu.roll(v, 32, 1)
                lane = lax.broadcasted_iota(jnp.int32, (8, 128), 1) // E
                chosen = [jnp.where(lane == g, v, 0.0) for g in range(4)]
                chosen = jnp.concatenate(chosen, axis=0).astype(bf16)
                rows = jnp.concatenate([star[:, 0, :], jnp.zeros((1, 128), f32)], axis=0)
                hi, lo = split(rows)
                rows = rows_for(chosen, hi) + rows_for(chosen, lo)
                rows = jnp.concatenate([rows, jnp.zeros((32, 64), f32)], axis=1)
                fixed_send[0:16] = rows[:16] + pltpu.roll(rows[16:], 64, 1)
                lane = lax.broadcasted_iota(jnp.int32, (1, 128), 1)
                fast = jnp.where(kind4 == 2, 1.0, 0.0).astype(f32)
                rows = jnp.concatenate(
                    [
                        plus[:, 0, :] * fast,
                        (lane % E).astype(f32),
                        (lane // E).astype(f32),
                        jnp.zeros((45, 128), f32),
                    ],
                    axis=0,
                )
                rows = rows_for(owed[...], jnp.concatenate(split(rows), axis=1))
                fixed_send[16:24] = rows[p * 8 : p * 8 + 8]

    def unpack_fixed():
        for p, there in far.items():

            @pl.when(there)
            def _():
                fixed(p).wait_send()
                fixed(p).wait_recv()
                row = lax.broadcasted_iota(jnp.int32, (32, 128), 0)
                lane = lax.broadcasted_iota(jnp.int32, (32, 128), 1)
                wide = (lane // E == row // 8) & (lane % E == p * 8 + row % 8)
                wide = jnp.where(wide, 1.0, 0.0).astype(f32).astype(bf16)
                rows = fixed_recv[0:16]
                rows = jnp.concatenate([rows, pltpu.roll(rows, 64, 1)], axis=0)
                rows = placed(rows, wide, 64)
                for r in range(63):
                    far_star[r] = jnp.broadcast_to(rows[r : r + 1], (8, 128))
                rows = fixed_recv[16:24]
                lane = lax.broadcasted_iota(jnp.int32, (8, 128), 1).astype(f32)
                element, face = rows[:, 81:82], rows[:, 82:83]
                owner = jnp.where(lane == element, 1.0, 0.0).astype(f32).astype(bf16)
                same = rows_for(owner, owner)
                order = lax.broadcasted_iota(jnp.int32, (8, 8), 1).astype(f32)
                leader = jnp.min(jnp.where(same > 0.5, order, 8.0), axis=1, keepdims=True)
                spot = jnp.where(lane == face * E + (p * 8) + leader, 1.0, 0.0).astype(f32)
                blank = [jnp.zeros((8, 128), f32)]
                spots = jnp.concatenate(blank * p + [spot] + blank * (3 - p), axis=0).astype(bf16)
                far_place[...] = jnp.concatenate([spots, spots], axis=1)
                rows = jnp.concatenate(blank * p + [rows] + blank * (3 - p), axis=0)
                rows = placed(rows, spots, 88)
                for r in range(81):
                    far_plus[r] = jnp.broadcast_to(rows[r : r + 1], (8, 128))

    def respond(u):
        mine = send_buf[u].reshape(32, 256)
        x = received(mine, far_place[:, 0:128], far_plus)
        both = project(expand(0, x, far_star))[1]
        answer[:, 0:224] = rows_for(far_place[...], both)

    def pair(h, _):
        u, v = 2 * h, 2 * h + 1
        total = expand(u, base[...], star)
        portion[...] = total
        traces, both = project(total)
        outgoing = rows_for(owed[...], both)
        for p in range(4):
            send_buf[u, p, :, 0:224] = outgoing[p * 8 : p * 8 + 8]

        @pl.when(h == 0)
        def _():
            pl.semaphore_wait(barrier, callers)

        by_relay = giver & (h == 0)

        @pl.when(by_relay)
        def _():
            hand_over(0).start()

        for p in (3, 2, 0, 1):
            there = links[p][0]

            @pl.when(there & jnp.logical_not(by_relay) if p == 3 else there)
            def _():
                send(u, p)

        @pl.when(h == 0)
        def _():
            late_tables()
            pack_fixed()

        @pl.when(by_relay)
        def _():
            hand_over(1).start()

        for p, there in far.items():

            @pl.when(there & (h == 0) & taker)
            def _():
                fixed(p).start()

        @pl.when(relay & (h == 0))
        def _():
            for part in range(2):
                hand_over(part).wait_recv()
                hand_on(part).start()

        stay(u, traces, both)

        @pl.when(relay & (h == 0))
        def _():
            hand_over(2).wait_recv()
            hand_on(2).start()

        inbox[...] = jnp.zeros_like(inbox)
        for p in range(4):

            @pl.when(near[p])
            def _():
                collect(u, p)
                inbox[p * 8 : p * 8 + 8] = recv_buf[u, p]

        absorb()

        @pl.when(is_far)
        def _():
            x = jnp.where(tall(mask[v]) > 0.5, base[...] + pending[...], base[...])
            early = rows_for(owed[...], project(expand(v, x, star))[1])
            for p, there in far.items():

                @pl.when(there)
                def _():
                    send_buf[v, p, :, 0:224] = early[p * 8 : p * 8 + 8]

                @pl.when(there & jnp.logical_not(by_relay) if p == 3 else there)
                def _():
                    send(v, p)

            @pl.when(by_relay)
            def _():
                hand_over(2).start()

            @pl.when(taker & (h > 0))
            def _():
                respond(u)

            inbox[...] = jnp.zeros_like(inbox)
            for p, there in far.items():

                @pl.when(there)
                def _():
                    collect(u, p)
                    inbox[p * 8 : p * 8 + 8] = recv_buf[u, p]

            absorb()

        x = jnp.where(tall(mask[v]) > 0.5, base[...] + pending[...], base[...])
        base[...] = x
        total = expand(v, x, star)
        portion[...] = total
        traces, both = project(total)
        outgoing = rows_for(owed[...], both)
        for p in range(4):

            @pl.when(near[p])
            def _():
                send_buf[v, p, :, 0:224] = outgoing[p * 8 : p * 8 + 8]
                send(v, p)

        stay(v, traces, both)
        inbox[...] = jnp.zeros_like(inbox)

        @pl.when(is_far)
        def _():
            @pl.when(h == 0)
            def _():
                unpack_fixed()

            @pl.when(giver | (h == 0))
            def _():
                respond(u)

            for p, there in far.items():

                @pl.when(there)
                def _():
                    collect(v, p)
                    rows = slice(p * 8, p * 8 + 8)
                    inbox[rows, 0:224] = recv_buf[v, p, :, 0:224] + answer[rows, 0:224]

        for p in range(4):

            @pl.when(near[p])
            def _():
                collect(v, p)
                inbox[p * 8 : p * 8 + 8] = recv_buf[v, p]

        absorb()
        last = h == STEPS // 2 - 1
        following = jnp.minimum(v + 1, STEPS - 1)
        ending = (tall(mask[following]) > 0.5) | last
        base[...] = jnp.where(ending, base[...] + pending[...], base[...])
        return 0

    lax.fori_loop(0, STEPS // 2, pair, 0)

    @pl.when(relay)
    def _():
        for part in range(3):
            hand_on(part).wait_send()

    out[...] = jnp.transpose(base[:, 0 : Q * E], (1, 0)).reshape(Q, E, M)


def on_device(dofs, jac, stiff, proj, root, plus_in, cluster, codes, send_faces):
    axes = (lax.axis_size("group"), lax.axis_size("dev"))
    scratch = [
        pltpu.VMEM((Q, E, M), f32),
        pltpu.VMEM((Q, Q, 3, E), f32),
        pltpu.VMEM((3, M, M), f32),
        pltpu.VMEM((21, 4, M), f32),
        pltpu.VMEM((Q, Q, 4, E), f32),
        pltpu.VMEM((Q, Q, 4, E), f32),
        pltpu.VMEM((1, E), jnp.int32),
        pltpu.VMEM((2, 4, E), jnp.int32),
        pltpu.SemaphoreType.DMA((8,)),
        pltpu.VMEM((63, 8, 128), f32),
        pltpu.VMEM((81, 8, 128), f32),
        pltpu.VMEM((81, 8, 128), f32),
        pltpu.VMEM((128, K3), bf16),
        pltpu.VMEM((8 * FM, 64), bf16),
        pltpu.VMEM((128, 4 * FM), bf16),
        pltpu.VMEM((4 * FM, 64), f32),
        pltpu.VMEM((STEPS * TERMS, 8, W), f32),
        pltpu.VMEM((STEPS, 8, W), f32),
        pltpu.VMEM((256, 128), bf16),
        pltpu.VMEM((32, 256), bf16),
        pltpu.VMEM((M, W), f32),
        pltpu.VMEM((M, W), f32),
        pltpu.VMEM((M, W), f32),
        pltpu.VMEM((32, 256), f32),
        pltpu.VMEM((STEPS, 4, 8, 256), f32),
        pltpu.VMEM((STEPS, 4, 8, 256), f32),
        pltpu.VMEM((24, 128), f32),
        pltpu.VMEM((24, 128), f32),
        pltpu.VMEM((63, 8, 128), f32),
        pltpu.VMEM((81, 8, 128), f32),
        pltpu.VMEM((32, 256), bf16),
        pltpu.VMEM((32, 256), f32),
        pltpu.SemaphoreType.DMA((STEPS, 4)),
        pltpu.SemaphoreType.DMA((STEPS, 4)),
        pltpu.SemaphoreType.DMA((2,)),
        pltpu.VMEM((2, 8, 256), f32),
        pltpu.VMEM((24, 128), f32),
        pltpu.SemaphoreType.DMA((3,)),
        pltpu.SemaphoreType.DMA((3,)),
    ]
    final = pl.pallas_call(
        functools.partial(kernel, axes),
        out_shape=jax.ShapeDtypeStruct((Q, E, M), f32),
        in_specs=[pl.BlockSpec(memory_space=pl.ANY)] * 8,
        out_specs=pl.BlockSpec(memory_space=pltpu.VMEM),
        scratch_shapes=scratch,
        compiler_params=pltpu.CompilerParams(collective_id=0, has_side_effects=True),
        name="lts_update",
    )(
        jnp.transpose(dofs, (1, 2, 0)),
        jnp.transpose(jac, (1, 2, 0, 3)),
        stiff,
        jnp.transpose(proj, (1, 0, 2)),
        jnp.transpose(root, (1, 2, 0, 3)),
        jnp.transpose(plus_in, (1, 2, 0, 3)),
        cluster.reshape(1, E),
        codes,
    )
    return jnp.transpose(final, (2, 0, 1))


def solution(mesh):
    placed = (
        P(None, None, ("group", "dev")),
        P(None, None, None, ("group", "dev")),
        P(),
        P(),
        P(None, None, None, ("group", "dev")),
        P(None, None, None, ("group", "dev")),
        P(("group", "dev")),
        P(None, None, ("group", "dev")),
        P(None, ("group", "dev")),
    )
    return jax.shard_map(
        on_device,
        mesh=mesh,
        in_specs=placed,
        out_specs=P(None, None, ("group", "dev")),
        check_vma=False,
    )
```

```python
import functools
import math

import jax
import jax.numpy as jnp
from jax import lax
from jax.experimental import pallas as pl
from jax.experimental.pallas import tpu as pltpu
from jax.sharding import PartitionSpec as P

TERMS = 6
STEPS = 4
MESH = pl.DeviceIdType.MESH
f32, bf16 = jnp.float32, jnp.bfloat16

M, Q, E, FM = 56, 9, 32, 24
W = 384
K3 = 176
TR = 216


def weights(power, offset):
    start, end = offset * 0.25, offset * 0.25 + 0.25
    return (end ** (power + 1) - start ** (power + 1)) / math.factorial(power + 1)


def split(x):
    hi = x.astype(bf16)
    return hi, (x - hi.astype(f32)).astype(bf16)


def stacked(x):
    return jnp.concatenate(split(x), axis=0)


def dot3(stack, x):
    rows = stack.shape[0] // 2
    hi, lo = split(x)
    both = jnp.dot(stack, hi, preferred_element_type=f32)
    return both[:rows] + both[rows:] + jnp.dot(stack[:rows], lo, preferred_element_type=f32)


def lane_group(rows):
    return lax.broadcasted_iota(jnp.int32, (rows, 128), 1) // E


def spread(v):
    group = lane_group(v.shape[0])
    odd, high = (group % 2) == 1, group >= 2
    even = jnp.where(odd, pltpu.roll(v, 32, 1), v)
    other = jnp.where(odd, v, pltpu.roll(v, 96, 1))
    even_r, other_r = pltpu.roll(even, 64, 1), pltpu.roll(other, 64, 1)
    return (
        jnp.where(high, even_r, even),
        jnp.where(high, other_r, other),
        jnp.where(high, even, even_r),
        jnp.where(high, other, other_r),
    )


def quad(stack, y):
    rows = stack.shape[0] // 2
    both = jnp.dot(stack, jnp.concatenate(split(y), axis=1), preferred_element_type=f32)
    return (both[:rows, :128] + both[rows:, :128]) + (both[:rows, 128:] + both[rows:, 128:])


def operator(x, star, s_stack):
    tiles = M // 8
    wide = []
    for tile in range(tiles):
        rows = x[tile * 8 : tile * 8 + 8]
        wide.append(
            (*spread(rows[:, :128]), *spread(rows[:, 128:256]), spread(rows[:, 256:])[0])
        )

    def weighted(tile, at):
        total = wide[tile][0] * star[at]
        for i in range(1, Q):
            total = total + wide[tile][i] * star[i * 7 + at]
        return total

    blank = [jnp.zeros((8, 128), f32)]
    last = [weighted(tile, 6) for tile in range(tiles)]
    rolled = [pltpu.roll(y, 96, 1) for y in last] + [pltpu.roll(y, 64, 1) for y in last]
    stack = s_stack[...]
    out = [quad(stack, jnp.concatenate(last + rolled + blank, axis=0))]
    for t in range(2):
        y = [weighted(tile, d * 2 + t) for d in range(3) for tile in range(tiles)]
        out.append(quad(stack, jnp.concatenate(y + blank, axis=0)))
    return jnp.concatenate([out[1][:M], out[2][:M], out[0][:M]], axis=1)


def to_face_lanes(t):
    group = lane_group(FM)
    out = []
    for q in range(Q):
        tile, g = q // 4, q % 4
        cut = slice(tile * 128, tile * 128 + 128)
        total = None
        for f in range(4):
            piece = t[f * FM : f * FM + FM, cut]
            piece = pltpu.roll(piece, (32 * (f - g)) % 128, 1) if f != g else piece
            total = piece if total is None else jnp.where(group == f, piece, total)
        out.append(total)
    return out


def to_quantity_lanes(flux):
    group = lane_group(FM)
    rows = []
    for f in range(4):
        lanes = []
        for t in range(3):
            total = jnp.zeros((FM, 128), f32)
            for j in range(4 * t, min(4 * t + 4, Q)):
                g = j % 4
                piece = pltpu.roll(flux[j], (32 * (g - f)) % 128, 1) if f != g else flux[j]
                total = jnp.where(group == g, piece, total)
            lanes.append(total)
        rows.append(jnp.concatenate(lanes, axis=1))
    return jnp.concatenate(rows, axis=0)


def contract(rows, table):
    out = []
    for j in range(Q):
        total = None
        for i in range(Q):
            left = rows[i].reshape(FM // 8, 8, 128)
            term = left * table[i * Q + j][None]
            total = term if total is None else total + term
        out.append(total.reshape(FM, 128))
    return out


def kernel(
    axes,
    *refs,
):
    inputs, (out, *refs) = refs[:8], refs[8:]
    held, copy_sem, refs = refs[:8], refs[8], refs[9:]
    copies = [pltpu.make_async_copy(a, b, copy_sem.at[i]) for i, (a, b) in enumerate(zip(inputs, held))]
    body(axes, copies, *held, out, *refs)


def body(
    axes,
    copies,
    dofs,
    jac,
    stiff,
    proj,
    root,
    plus_in,
    cluster,
    codes,
    out,
    star,
    minus,
    plus,
    s_stack,
    p_stack,
    pt_stack,
    p_rows,
    coef,
    mask,
    pick,
    owed,
    base,
    portion,
    pending,
    inbox,
    send_buf,
    recv_buf,
    fixed_send,
    fixed_recv,
    far_star,
    far_plus,
    far_place,
    answer,
    send_sem,
    recv_sem,
    fixed_sem,
    relay_rows,
    relay_fixed,
    relay_sem,
    onward_sem,
):
    group, dev = lax.axis_index("group"), lax.axis_index("dev")
    n_group, n_dev = axes
    half = n_dev // 2
    links = (
        (group > 0, {"group": group - 1}, 1),
        (group < n_group - 1, {"group": group + 1}, 0),
        (dev > 0, {"dev": dev - 1}, 3),
        (dev < n_dev - 1, {"dev": dev + 1}, 2),
    )
    far = {2: dev == half, 3: dev == half - 1}
    is_far = (dev == half) | (dev == half - 1)
    near = [links[0][0], links[1][0], (dev > 0) & (dev != half)]
    near.append((dev < n_dev - 1) & (dev != half - 1))
    middle = n_group // 2
    giver = (dev == half - 1) & (group < middle)
    taker = (dev == half) & (group < middle)
    relay = (dev == half - 2) & (group >= middle)
    opposite = lax.rem(group + middle, n_group)
    barrier = pltpu.get_barrier_semaphore()

    def greet(there, peer):
        @pl.when(there)
        def _():
            pl.semaphore_signal(barrier, inc=1, device_id=peer, device_id_type=MESH)

    for p, (there, peer, _) in enumerate(links):
        greet(there & jnp.logical_not(taker) if p == 2 else there, peer)
    above = {"group": opposite, "dev": half - 2 + 4 * lax.div(group, middle)}
    greet(giver | taker, above)
    greet(relay, {"group": opposite, "dev": half - 1})
    greet(relay, {"group": opposite, "dev": half})
    callers = sum(there.astype(jnp.int32) for there, _, _ in links)
    callers = callers + taker.astype(jnp.int32) + 2 * relay.astype(jnp.int32)

    for copy in copies:
        copy.start()
    send_buf[...] = jnp.zeros_like(send_buf)
    fixed_send[...] = jnp.zeros_like(fixed_send)

    for copy in copies:
        copy.wait()

    kind = cluster[...]
    rate = jnp.where(kind == 2, 4.0, jnp.where(kind == 1, 2.0, 1.0)).astype(f32)
    rate4 = jnp.concatenate([rate] * 4, axis=1)
    kind4 = jnp.concatenate([kind] * 4, axis=1)
    kind12 = jnp.broadcast_to(jnp.concatenate([kind4] * 3, axis=1), (8, W))
    last = [[] for _ in range(Q)]
    for d in range(3):
        for i in range(Q):
            row = [
                0.5 * rate * (jac[i, j, d : d + 1, :] + jac[j, i, d : d + 1, :]) for j in range(Q)
            ]
            last[i].append(row[8])
            for t in range(2):
                tile = jnp.concatenate(row[4 * t : 4 * t + 4], axis=1)
                star[i * 7 + d * 2 + t] = jnp.broadcast_to(tile, (8, 128))
    for i in range(Q):
        tile = jnp.concatenate(last[i] + [jnp.zeros((1, E), f32)], axis=1)
        star[i * 7 + 6] = jnp.broadcast_to(tile, (8, 128))
    def late_tables():
        roots = []
        for i in range(Q):
            roots.append(jnp.concatenate([root[i, :, f, :] for f in range(4)], axis=1))
            row = jnp.concatenate([plus_in[i, :, f, :] for f in range(4)], axis=1) * rate4
            for j in range(Q):
                plus[i * Q + j] = jnp.broadcast_to(row[j : j + 1], (8, 128))
        for i in range(Q):
            for j in range(i, Q):
                row = jnp.sum(roots[i] * roots[j], axis=0, keepdims=True) * rate4
                row = jnp.broadcast_to(row, (8, 128))
                minus[i * Q + j] = row
                minus[j * Q + i] = row
        local = lax.broadcasted_iota(jnp.int32, (128, 128), 0) == code
        local = jnp.where(local, 1.0, 0.0).astype(f32).astype(bf16)
        pick[...] = jnp.concatenate([local, local], axis=0)
        pt_stack[...] = stacked(jnp.transpose(p_rows[...], (1, 0)))
        pending[...] = jnp.zeros_like(pending)
        for u in range(STEPS):
            starting = (True, fast, fast | middling, fast)[u]
            mask[u] = jnp.where(starting, 1.0, 0.0).astype(f32) if u else jnp.ones((8, W), f32)

    stiff_rows = [stiff[d] - jnp.transpose(stiff[d], (1, 0)) for d in range(3)]
    stiff_rows = jnp.concatenate(stiff_rows + [jnp.zeros((M, K3 - 3 * M), f32)], axis=1)
    s_stack[...] = stacked(jnp.concatenate([stiff_rows, jnp.zeros((8, K3), f32)], axis=0))
    p_rows[...] = jnp.zeros_like(p_rows)
    for f in range(4):
        p_rows[f * FM : f * FM + 21, 0:M] = proj[:, f, :]
    p_stack[...] = stacked(p_rows[...])
    fast, middling = kind12 == 2, kind12 == 1
    for u in range(STEPS):
        for k in range(TERMS):
            coef[u * TERMS + k] = jnp.where(
                fast,
                weights(k, 0),
                jnp.where(middling, weights(k, u % 2), weights(k, u)),
            ).astype(f32)
    code = jnp.concatenate([codes[0, f : f + 1, :] for f in range(4)], axis=1)
    remote = lax.broadcasted_iota(jnp.int32, (32, 128), 0) + 128 == code
    remote = jnp.where(remote, 1.0, 0.0).astype(f32).astype(bf16)
    owed[...] = jnp.concatenate([remote, remote], axis=1)
    base[...] = jnp.zeros_like(base)
    base[:, 0 : Q * E] = jnp.transpose(dofs[...].reshape(Q * E, M), (1, 0))

    def tall(row):
        return jnp.broadcast_to(row[None], (M // 8, 8, W)).reshape(M, W)

    def exchange(u, p, slot):
        return pltpu.make_async_remote_copy(
            src_ref=send_buf.at[u, p],
            dst_ref=recv_buf.at[u, slot],
            send_sem=send_sem.at[u, p],
            recv_sem=recv_sem.at[u, slot],
            device_id=links[p][1],
            device_id_type=MESH,
        )

    def send(u, p):
        exchange(u, p, links[p][2]).start()

    def collect(u, p):
        exchange(u, p, links[p][2]).wait_send()
        exchange(u, p, p).wait_recv()

    def fixed(p):
        return pltpu.make_async_remote_copy(
            src_ref=fixed_send,
            dst_ref=fixed_recv,
            send_sem=fixed_sem.at[0],
            recv_sem=fixed_sem.at[1],
            device_id=links[p][1],
            device_id_type=MESH,
        )

    def hand_over(part):
        return pltpu.make_async_remote_copy(
            src_ref=(send_buf.at[0, 3], fixed_send, send_buf.at[1, 3])[part],
            dst_ref=(relay_rows.at[0], relay_fixed, relay_rows.at[1])[part],
            send_sem=(send_sem.at[0, 3], fixed_sem.at[0], send_sem.at[1, 3])[part],
            recv_sem=relay_sem.at[part],
            device_id=above,
            device_id_type=MESH,
        )

    def hand_on(part):
        return pltpu.make_async_remote_copy(
            src_ref=(relay_rows.at[0], relay_fixed, relay_rows.at[1])[part],
            dst_ref=(recv_buf.at[0, 2], fixed_recv, recv_buf.at[1, 2])[part],
            send_sem=onward_sem.at[part],
            recv_sem=(recv_sem.at[0, 2], fixed_sem.at[1], recv_sem.at[1, 2])[part],
            device_id={"group": opposite, "dev": half},
            device_id_type=MESH,
        )

    def expand(u, x, table):
        def term(k, carry):
            x, total = carry
            x = operator(x, table, s_stack)
            return x, total + tall(coef[u * TERMS + k]) * x

        return lax.fori_loop(1, TERMS, term, (x, tall(coef[u * TERMS]) * x), unroll=True)[1]

    def project(total):
        padded = jnp.concatenate([total, jnp.zeros((8, W), f32)], axis=0)
        traces = to_face_lanes(dot3(p_stack[...], padded))
        rows = jnp.concatenate(traces + [jnp.zeros((8, 128), f32)], axis=0)
        return traces, jnp.concatenate(split(rows), axis=1)

    def rows_for(places, both):
        return lax.dot_general(
            places, both, (((1,), (1,)), ((), ())), preferred_element_type=f32
        )

    def lifted(flux):
        return dot3(pt_stack[...], to_quantity_lanes(flux))[:M]

    def placed(rows, places, count):
        hi, lo = split(jnp.transpose(rows, (1, 0))[:count])
        return jnp.dot(hi, places, preferred_element_type=f32) + jnp.dot(
            lo, places, preferred_element_type=f32
        )

    def received(rows, places, table):
        taken = placed(rows, places, 224)
        return lifted(contract([taken[q * FM : q * FM + FM] for q in range(Q)], table))

    def absorb():
        pending[...] += received(inbox[...], owed[:, 0:128], plus)

    def stay(u, traces, both):
        taken = jnp.dot(both, pick[...], preferred_element_type=f32)
        taken = [taken[q * FM : q * FM + FM] for q in range(Q)]
        flux = [a - b for a, b in zip(contract(taken, plus), contract(traces, minus))]
        pending[...] = (
            jnp.where(tall(mask[u]) > 0.5, 0.0, pending[...])
            + operator(portion[...], star, s_stack)
            + lifted(flux)
        )

    def pack_fixed():
        for p, there in far.items():

            @pl.when(there)
            def _():
                v = owed[:, 0:128].astype(f32)[p * 8 : p * 8 + 8]
                v = v + pltpu.roll(v, 64, 1)
                v = v + pltpu.roll(v, 32, 1)
                lane = lax.broadcasted_iota(jnp.int32, (8, 128), 1) // E
                chosen = [jnp.where(lane == g, v, 0.0) for g in range(4)]
                chosen = jnp.concatenate(chosen, axis=0).astype(bf16)
                rows = jnp.concatenate([star[:, 0, :], jnp.zeros((1, 128), f32)], axis=0)
                hi, lo = split(rows)
                rows = rows_for(chosen, hi) + rows_for(chosen, lo)
                rows = jnp.concatenate([rows, jnp.zeros((32, 64), f32)], axis=1)
                fixed_send[0:16] = rows[:16] + pltpu.roll(rows[16:], 64, 1)
                lane = lax.broadcasted_iota(jnp.int32, (1, 128), 1)
                fast = jnp.where(kind4 == 2, 1.0, 0.0).astype(f32)
                rows = jnp.concatenate(
                    [
                        plus[:, 0, :] * fast,
                        (lane % E).astype(f32),
                        (lane // E).astype(f32),
                        jnp.zeros((45, 128), f32),
                    ],
                    axis=0,
                )
                rows = rows_for(owed[...], jnp.concatenate(split(rows), axis=1))
                fixed_send[16:24] = rows[p * 8 : p * 8 + 8]

    def unpack_fixed():
        for p, there in far.items():

            @pl.when(there)
            def _():
                fixed(p).wait_send()
                fixed(p).wait_recv()
                row = lax.broadcasted_iota(jnp.int32, (32, 128), 0)
                lane = lax.broadcasted_iota(jnp.int32, (32, 128), 1)
                wide = (lane // E == row // 8) & (lane % E == p * 8 + row % 8)
                wide = jnp.where(wide, 1.0, 0.0).astype(f32).astype(bf16)
                rows = fixed_recv[0:16]
                rows = jnp.concatenate([rows, pltpu.roll(rows, 64, 1)], axis=0)
                rows = placed(rows, wide, 64)
                for r in range(63):
                    far_star[r] = jnp.broadcast_to(rows[r : r + 1], (8, 128))
                rows = fixed_recv[16:24]
                lane = lax.broadcasted_iota(jnp.int32, (8, 128), 1).astype(f32)
                element, face = rows[:, 81:82], rows[:, 82:83]
                owner = jnp.where(lane == element, 1.0, 0.0).astype(f32).astype(bf16)
                same = rows_for(owner, owner)
                order = lax.broadcasted_iota(jnp.int32, (8, 8), 1).astype(f32)
                leader = jnp.min(jnp.where(same > 0.5, order, 8.0), axis=1, keepdims=True)
                spot = jnp.where(lane == face * E + (p * 8) + leader, 1.0, 0.0).astype(f32)
                blank = [jnp.zeros((8, 128), f32)]
                spots = jnp.concatenate(blank * p + [spot] + blank * (3 - p), axis=0).astype(bf16)
                far_place[...] = jnp.concatenate([spots, spots], axis=1)
                rows = jnp.concatenate(blank * p + [rows] + blank * (3 - p), axis=0)
                rows = placed(rows, spots, 88)
                for r in range(81):
                    far_plus[r] = jnp.broadcast_to(rows[r : r + 1], (8, 128))

    def respond(u):
        mine = send_buf[u].reshape(32, 256)
        x = received(mine, far_place[:, 0:128], far_plus)
        both = project(expand(0, x, far_star))[1]
        answer[:, 0:224] = rows_for(far_place[...], both)

    def pair(h, _):
        u, v = 2 * h, 2 * h + 1
        total = expand(u, base[...], star)
        portion[...] = total
        traces, both = project(total)
        outgoing = rows_for(owed[...], both)
        for p in range(4):
            send_buf[u, p, :, 0:224] = outgoing[p * 8 : p * 8 + 8]

        @pl.when(h == 0)
        def _():
            pl.semaphore_wait(barrier, callers)

        by_relay = giver & (h == 0)

        @pl.when(by_relay)
        def _():
            hand_over(0).start()

        for p in (3, 2, 0, 1):
            there = links[p][0]

            @pl.when(there & jnp.logical_not(by_relay) if p == 3 else there)
            def _():
                send(u, p)

        @pl.when(h == 0)
        def _():
            late_tables()
            pack_fixed()

        @pl.when(by_relay)
        def _():
            hand_over(1).start()

        for p, there in far.items():

            @pl.when(there & (h == 0) & jnp.logical_not(giver))
            def _():
                fixed(p).start()

        @pl.when(relay & (h == 0))
        def _():
            for part in range(2):
                hand_over(part).wait_recv()
                hand_on(part).start()

        stay(u, traces, both)

        @pl.when(relay & (h == 0))
        def _():
            hand_over(2).wait_recv()
            hand_on(2).start()

        inbox[...] = jnp.zeros_like(inbox)
        for p in range(4):

            @pl.when(near[p])
            def _():
                collect(u, p)
                inbox[p * 8 : p * 8 + 8] = recv_buf[u, p]

        absorb()

        @pl.when(is_far)
        def _():
            x = jnp.where(tall(mask[v]) > 0.5, base[...] + pending[...], base[...])
            early = rows_for(owed[...], project(expand(v, x, star))[1])
            for p, there in far.items():

                @pl.when(there)
                def _():
                    send_buf[v, p, :, 0:224] = early[p * 8 : p * 8 + 8]

                @pl.when(there & jnp.logical_not(by_relay) if p == 3 else there)
                def _():
                    send(v, p)

            @pl.when(by_relay)
            def _():
                hand_over(2).start()

            @pl.when(h > 0)
            def _():
                respond(u)

            inbox[...] = jnp.zeros_like(inbox)
            for p, there in far.items():

                @pl.when(there)
                def _():
                    collect(u, p)
                    inbox[p * 8 : p * 8 + 8] = recv_buf[u, p]

            absorb()

        x = jnp.where(tall(mask[v]) > 0.5, base[...] + pending[...], base[...])
        base[...] = x
        total = expand(v, x, star)
        portion[...] = total
        traces, both = project(total)
        outgoing = rows_for(owed[...], both)
        for p in range(4):

            @pl.when(near[p])
            def _():
                send_buf[v, p, :, 0:224] = outgoing[p * 8 : p * 8 + 8]
                send(v, p)

        stay(v, traces, both)
        inbox[...] = jnp.zeros_like(inbox)

        @pl.when(is_far)
        def _():
            @pl.when(h == 0)
            def _():
                unpack_fixed()

            @pl.when(h == 0)
            def _():
                respond(u)

            for p, there in far.items():

                @pl.when(there)
                def _():
                    collect(v, p)
                    rows = slice(p * 8, p * 8 + 8)
                    inbox[rows, 0:224] = recv_buf[v, p, :, 0:224] + answer[rows, 0:224]

        for p in range(4):

            @pl.when(near[p])
            def _():
                collect(v, p)
                inbox[p * 8 : p * 8 + 8] = recv_buf[v, p]

        absorb()
        last = h == STEPS // 2 - 1
        following = jnp.minimum(v + 1, STEPS - 1)
        ending = (tall(mask[following]) > 0.5) | last
        base[...] = jnp.where(ending, base[...] + pending[...], base[...])
        return 0

    lax.fori_loop(0, STEPS // 2, pair, 0)

    @pl.when(relay)
    def _():
        for part in range(3):
            hand_on(part).wait_send()

    out[...] = jnp.transpose(base[:, 0 : Q * E], (1, 0)).reshape(Q, E, M)


def on_device(dofs, jac, stiff, proj, root, plus_in, cluster, codes, send_faces):
    axes = (lax.axis_size("group"), lax.axis_size("dev"))
    scratch = [
        pltpu.VMEM((Q, E, M), f32),
        pltpu.VMEM((Q, Q, 3, E), f32),
        pltpu.VMEM((3, M, M), f32),
        pltpu.VMEM((21, 4, M), f32),
        pltpu.VMEM((Q, Q, 4, E), f32),
        pltpu.VMEM((Q, Q, 4, E), f32),
        pltpu.VMEM((1, E), jnp.int32),
        pltpu.VMEM((2, 4, E), jnp.int32),
        pltpu.SemaphoreType.DMA((8,)),
        pltpu.VMEM((63, 8, 128), f32),
        pltpu.VMEM((81, 8, 128), f32),
        pltpu.VMEM((81, 8, 128), f32),
        pltpu.VMEM((128, K3), bf16),
        pltpu.VMEM((8 * FM, 64), bf16),
        pltpu.VMEM((128, 4 * FM), bf16),
        pltpu.VMEM((4 * FM, 64), f32),
        pltpu.VMEM((STEPS * TERMS, 8, W), f32),
        pltpu.VMEM((STEPS, 8, W), f32),
        pltpu.VMEM((256, 128), bf16),
        pltpu.VMEM((32, 256), bf16),
        pltpu.VMEM((M, W), f32),
        pltpu.VMEM((M, W), f32),
        pltpu.VMEM((M, W), f32),
        pltpu.VMEM((32, 256), f32),
        pltpu.VMEM((STEPS, 4, 8, 256), f32),
        pltpu.VMEM((STEPS, 4, 8, 256), f32),
        pltpu.VMEM((24, 128), f32),
        pltpu.VMEM((24, 128), f32),
        pltpu.VMEM((63, 8, 128), f32),
        pltpu.VMEM((81, 8, 128), f32),
        pltpu.VMEM((32, 256), bf16),
        pltpu.VMEM((32, 256), f32),
        pltpu.SemaphoreType.DMA((STEPS, 4)),
        pltpu.SemaphoreType.DMA((STEPS, 4)),
        pltpu.SemaphoreType.DMA((2,)),
        pltpu.VMEM((2, 8, 256), f32),
        pltpu.VMEM((24, 128), f32),
        pltpu.SemaphoreType.DMA((3,)),
        pltpu.SemaphoreType.DMA((3,)),
    ]
    final = pl.pallas_call(
        functools.partial(kernel, axes),
        out_shape=jax.ShapeDtypeStruct((Q, E, M), f32),
        in_specs=[pl.BlockSpec(memory_space=pl.ANY)] * 8,
        out_specs=pl.BlockSpec(memory_space=pltpu.VMEM),
        scratch_shapes=scratch,
        compiler_params=pltpu.CompilerParams(collective_id=0, has_side_effects=True),
        name="lts_update",
    )(
        jnp.transpose(dofs, (1, 2, 0)),
        jnp.transpose(jac, (1, 2, 0, 3)),
        stiff,
        jnp.transpose(proj, (1, 0, 2)),
        jnp.transpose(root, (1, 2, 0, 3)),
        jnp.transpose(plus_in, (1, 2, 0, 3)),
        cluster.reshape(1, E),
        codes,
    )
    return jnp.transpose(final, (2, 0, 1))


def solution(mesh):
    placed = (
        P(None, None, ("group", "dev")),
        P(None, None, None, ("group", "dev")),
        P(),
        P(),
        P(None, None, None, ("group", "dev")),
        P(None, None, None, ("group", "dev")),
        P(("group", "dev")),
        P(None, None, ("group", "dev")),
        P(None, ("group", "dev")),
    )
    return jax.shard_map(
        on_device,
        mesh=mesh,
        in_specs=placed,
        out_specs=P(None, None, ("group", "dev")),
        check_vma=False,
    )
```
